512 devices in a mesh: member: 8 (over z_lo, core), tile: 64 (over z_hi, x, y).
Axes of the slice: x: 4, y: 8, z: 8 (z_hi: 2, z_lo: 4; z = z_hi * 4 + z_lo), core: 2. Of those that a mesh axis runs over, the one named last changes fastest.
Arguments:
- inputs: bfloat16 [8, 32768, 512], P('member', 'tile'), may hold values from -6 to 6
- noise: bfloat16 [8, 32768, 128], P('member', 'tile'), may hold values from -6 to 6
- neighbours: int32 [8, 32768], P(None, 'tile'), may hold values from 0 to 639, as said below
- region_map: int32 [64], P('tile'), may hold values from 0 to 7, as said below
- msg_weight: bfloat16 [512, 512], replicated, may hold values from -0.25 to 0.25
- up_weight: bfloat16 [512, 1024], replicated, may hold values from -0.25 to 0.25
- down_weight: bfloat16 [1024, 512], replicated, may hold values from -0.1875 to 0.1875
- student_in: bfloat16 [512, 512], replicated, may hold values from -0.25 to 0.25
- student_noise: bfloat16 [128, 512], replicated, may hold values from -0.5 to 0.5
- student_out: bfloat16 [512, 512], replicated, may hold values from -0.25 to 0.25
Outputs:
- teacher_out: bfloat16 [8, 32768, 512], P('member', 'tile')
- region_loss: float32 [8], replicated
- grad_in: float32 [512, 512], P('tile')
- grad_noise: float32 [128, 512], P('tile')
- grad_out: float32 [512, 512], P('tile')
The draws below stay inside these ranges and needn't reach their ends.
Inputs may be any that keep to these rules, and one draw needn't show every extreme that they name: `neighbours`: each index lies within 64 of the cell's own row (its row plus 64); the first index of a tile's first cell is 0 and that of its last cell is 639. `region_map`: each region holds 8 tiles.
All inputs are finite; a program needn't handle non-finite values.
Results may differ from the reference program's by a relative error of at most 0.0039.
The reference program's roundings to bfloat16 on the way (of `gathered`, `normed`, `hidden`, `shidden`, `student`, `gstudent` and `gpre`) count: a program that leaves them out, or rounds other values in their place, can miss the bound.
Values may be sent and summed in bfloat16 or wider, within the bound.
No kernel may reach another device: no remote copies, remote signals or barrier semaphores. Data moves between devices by JAX's collectives and lax.ppermute only.
A program may use at most 64 MiB of HBM per device.

```python
import math
import jax
import jax.numpy as jnp
from jax import lax

D = 512
FF = 1024
H = 512
NOISE = 128
NBRS = 8
HALO = 64
REGIONS = 8
CELLS = 512
MEMBERS = 8
TILES = 64
CELLS_ALL = 32768


def draw_neighbours(key, part):
    offsets = jax.random.randint(key, (NBRS, CELLS_ALL), -HALO, HALO + 1).astype(jnp.int32)
    local = jnp.arange(CELLS_ALL, dtype=jnp.int32) % CELLS
    indices = local[None, :] + HALO + offsets
    first_row = jnp.where(local == 0, 0, jnp.where(local == CELLS - 1, CELLS + 2 * HALO - 1, indices[0]))
    return indices.at[0].set(first_row).astype(jnp.int32)


def draw_region_map(key, part):
    order = jax.random.permutation(key, TILES)
    return (order % REGIONS).astype(jnp.int32)


def steps_of(rng, shape, pieces, low, high):
    level = 1.0
    for axis_at, shards_of in pieces:
        heights = jax.random.uniform(jax.random.fold_in(jax.random.fold_in(rng, 6), axis_at), (shards_of,), jnp.float32, low / len(pieces), high / len(pieces))
        level = level * jnp.repeat(jnp.exp(heights), shape[axis_at] // shards_of).reshape((-1,) + (1,) * (len(shape) - 1 - axis_at))
    return level


def bell_draw(own_key, dims, deviation, most, cuts=(), held_as=jnp.bfloat16):
    loudness = steps_of(own_key, dims, cuts, -0.22, 0.18) if cuts else 1.0
    drawn = jax.random.normal(own_key, dims, jnp.float32) * deviation * loudness
    return jnp.minimum(jnp.maximum(drawn, -most), most).astype(held_as)


def setup_inputs(seed: int = 0) -> dict:
    splits = jax.random.split(jax.random.key(seed), 11)
    inputs = bell_draw(splits[0], (MEMBERS, CELLS_ALL, D), 1.0, 6.0, ((0, 8), (1, 64)))
    noise = bell_draw(splits[1], (MEMBERS, CELLS_ALL, NOISE), 1.0, 6.0, ((0, 8), (1, 64)))
    neighbours = draw_neighbours(jax.random.fold_in(splits[10], 71), 0)
    region_map = draw_region_map(jax.random.fold_in(splits[10], 71), 0)
    msg_weight = bell_draw(splits[4], (D, D), D ** -0.5, 0.25)
    up_weight = bell_draw(splits[5], (D, FF), D ** -0.5, 0.25)
    down_weight = bell_draw(splits[6], (FF, D), FF ** -0.5, 0.1875)
    student_in = bell_draw(splits[7], (D, H), D ** -0.5, 0.25)
    student_noise = bell_draw(splits[8], (NOISE, H), NOISE ** -0.5, 0.5)
    student_out = bell_draw(splits[9], (H, D), H ** -0.5, 0.25)
    return dict(inputs=inputs, noise=noise, neighbours=neighbours, region_map=region_map, msg_weight=msg_weight, up_weight=up_weight, down_weight=down_weight, student_in=student_in, student_noise=student_noise, student_out=student_out)


def smooth(diff):
    return jnp.sqrt(diff * diff + 0.01) - 0.1

def smooth_grad(diff):
    return diff / jnp.sqrt(diff * diff + 0.01)

def silu_grad(value):
    sig = jax.nn.sigmoid(value)
    return sig * (1.0 + value * (1.0 - sig))

def reference(inputs, noise, neighbours, region_map, msg_weight, up_weight, down_weight, student_in, student_noise, student_out):
    members = MEMBERS
    cell_ids = jnp.arange(CELLS_ALL, dtype=jnp.int32)
    cell_tile = cell_ids // CELLS
    padded_ids = (cell_tile[None, :] * CELLS + neighbours).astype(jnp.int32)

    def teacher(state):
        padded = jnp.pad(state, ((HALO, HALO), (0, 0)))
        total = jnp.zeros((CELLS_ALL, D), jnp.float32)
        for column in range(NBRS):
            total = total + padded[padded_ids[column]].astype(jnp.float32)
        gathered = (total / NBRS).astype(jnp.bfloat16)
        resid = state.astype(jnp.float32) + jnp.dot(gathered, msg_weight, preferred_element_type=jnp.float32)
        normed = (resid * lax.rsqrt(lax.optimization_barrier(jnp.mean(resid * resid, axis=1, keepdims=True)) + 1e-06)).astype(jnp.bfloat16)
        hidden = jax.nn.silu(jnp.dot(normed, up_weight, preferred_element_type=jnp.float32)).astype(jnp.bfloat16)
        return (resid + jnp.dot(hidden, down_weight, preferred_element_type=jnp.float32)).astype(jnp.bfloat16)
    teacher_out = lax.map(teacher, inputs)

    def forward(pair):
        state, draws = pair
        preact = jnp.dot(state, student_in, preferred_element_type=jnp.float32) + jnp.dot(draws, student_noise, preferred_element_type=jnp.float32)
        shidden = jax.nn.silu(preact).astype(jnp.bfloat16)
        return (state.astype(jnp.float32) + jnp.dot(shidden, student_out, preferred_element_type=jnp.float32)).astype(jnp.bfloat16)
    student = lax.map(forward, (inputs, noise))
    s_all = student.astype(jnp.float32)
    t_all = teacher_out.astype(jnp.float32)

    def visit(carry, other):
        grads, losses = carry
        other_s, other_t = other
        cross = s_all - other_t[None]
        within = s_all - other_s[None]
        grads = grads + smooth_grad(cross) / (members * members) - smooth_grad(within) / (members * (members - 1))
        losses = losses + lax.optimization_barrier(jnp.sum(smooth(cross) / (members * members) - smooth(within) / (2 * members * (members - 1)), axis=(0, 2)))
        return ((grads, losses), None)
    start = (jnp.zeros_like(s_all), jnp.zeros((CELLS_ALL,), jnp.float32))
    (grads, crps), _ = lax.scan(visit, start, (s_all, t_all))
    gstudent = (grads * (1.0 / math.sqrt(CELLS_ALL))).astype(jnp.bfloat16)
    tile_sums = lax.optimization_barrier(jnp.sum(crps.reshape(TILES, CELLS), axis=1))
    onehot = (region_map[:, None] == jnp.arange(REGIONS, dtype=jnp.int32)[None, :]).astype(jnp.float32)
    region_loss = lax.optimization_barrier(jnp.sum(onehot * tile_sums[:, None], axis=0)) / (CELLS_ALL // REGIONS * D)

    def backward(carry, item):
        acc_in, acc_noise, acc_out = carry
        state, draws, gmember = item
        preact = jnp.dot(state, student_in, preferred_element_type=jnp.float32) + jnp.dot(draws, student_noise, preferred_element_type=jnp.float32)
        shidden = jax.nn.silu(preact).astype(jnp.bfloat16)
        acc_out = acc_out + jnp.dot(shidden.T, gmember, preferred_element_type=jnp.float32)
        gpre = (jnp.dot(gmember, student_out.T, preferred_element_type=jnp.float32) * silu_grad(preact)).astype(jnp.bfloat16)
        acc_in = acc_in + jnp.dot(state.T, gpre, preferred_element_type=jnp.float32)
        acc_noise = acc_noise + jnp.dot(draws.T, gpre, preferred_element_type=jnp.float32)
        return ((acc_in, acc_noise, acc_out), None)
    zeros = (jnp.zeros((D, H), jnp.float32), jnp.zeros((NOISE, H), jnp.float32), jnp.zeros((H, D), jnp.float32))
    (grad_in, grad_noise, grad_out), _ = lax.scan(backward, zeros, (inputs, noise, gstudent))
    return (teacher_out, region_loss, grad_in, grad_noise, grad_out)
```

```python
import math

import jax
import jax.numpy as jnp
from jax import lax
from jax.experimental import pallas as pl
from jax.experimental.pallas import tpu as pltpu
from jax.sharding import Mesh
from jax.sharding import PartitionSpec as P

D = 512
FF = 1024
H = 512
NOISE = 128
NBRS = 8
HALO = 64
REGIONS = 8
MEMBERS = 8
CELLS = 512
BLOCK = CELLS // MEMBERS
CELLS_ALL = 32768
TILES = 64
HALF = D // 2
SHARE = 40
LOSS_ROW = 36

MEMBER = ("member_0", "core")
TILE = ("tile_0", "tile_1", "tile_2")
BF16 = jnp.bfloat16
F32 = jnp.float32


def teacher_kernel(top, state, bottom, near, msg, up, down, out, ext):
    ext[0:HALO] = top[...]
    ext[HALO : HALO + CELLS] = state[...]
    ext[HALO + CELLS :] = bottom[...]
    rows = 256
    sub = 128
    for at in range(0, CELLS, rows):
        parts = []
        for start in range(at, at + rows, sub):
            picks = near[:, start : start + sub].T
            lanes = lax.broadcasted_iota(jnp.int32, (sub, 2 * sub), 1) + start
            count = jnp.zeros((sub, 2 * sub), F32)
            for k in range(NBRS):
                count = count + jnp.where(picks[:, k : k + 1] == lanes, 1.0 / NBRS, 0.0)
            parts.append(
                jnp.dot(
                    count.astype(BF16),
                    ext[start : start + 2 * sub],
                    preferred_element_type=F32,
                ).astype(BF16)
            )
        gathered = jnp.concatenate(parts, axis=0)
        resid = state[at : at + rows].astype(F32) + jnp.dot(
            gathered, msg[...], preferred_element_type=F32
        )
        power = jnp.mean(resid * resid, axis=1, keepdims=True)
        normed = (resid * lax.rsqrt(power + 1e-06)).astype(BF16)
        hidden = jax.nn.silu(jnp.dot(normed, up[...], preferred_element_type=F32)).astype(BF16)
        out[at : at + rows] = (
            resid + jnp.dot(hidden, down[...], preferred_element_type=F32)
        ).astype(BF16)


def student_kernel(both, w_in, w_noise, w_out, student, shidden, slope):
    rows = 256
    for at in range(0, CELLS, rows):
        state = both[at : at + rows, :D]
        draws = both[at : at + rows, D:]
        preact = jnp.dot(state, w_in[...], preferred_element_type=F32) + jnp.dot(
            draws, w_noise[...], preferred_element_type=F32
        )
        sig = jax.nn.sigmoid(preact)
        hid = (preact * sig).astype(BF16)
        shidden[at : at + rows] = hid
        slope[at : at + rows] = sig * (1.0 + preact * (1.0 - sig))
        student[at : at + rows] = (
            state.astype(F32) + jnp.dot(hid, w_out[...], preferred_element_type=F32)
        ).astype(BF16)


def score_kernel(student, teacher, both, shidden, slope, w_out, place, grads, gst, wide):
    step = 16
    wide[...] = jnp.zeros_like(wide)

    def block(cell, lane):
        s = [student[m, pl.ds(cell, step), lane : lane + 128].astype(F32) for m in range(MEMBERS)]
        g = [jnp.zeros((step, 128), F32) for _ in range(MEMBERS)]
        loss = jnp.zeros((step, 128), F32)
        for n in range(MEMBERS):
            t = teacher[n, pl.ds(cell, step), lane : lane + 128].astype(F32)
            for m in range(MEMBERS):
                d = s[m] - t
                q = d * d + 0.01
                inv = lax.rsqrt(q)
                loss = loss + q * inv
                g[m] = g[m] + d * inv
        ratio = (MEMBERS - 1) / MEMBERS
        loss = loss * ratio
        g = [x * ratio for x in g]
        for m in range(MEMBERS):
            for n in range(m + 1, MEMBERS):
                d = s[m] - s[n]
                q = d * d + 0.01
                inv = lax.rsqrt(q)
                r = d * inv
                loss = loss - q * inv
                g[m] = g[m] - r
                g[n] = g[n] + r
        scale = 1.0 / (MEMBERS * (MEMBERS - 1) * math.sqrt(CELLS_ALL))
        for m in range(MEMBERS):
            gst[m, pl.ds(cell, step), lane : lane + 128] = (g[m] * scale).astype(BF16)
        pairs = MEMBERS * (MEMBERS - 1)
        wide[...] += (loss - 0.1 * (pairs - pairs // 2)) * (1.0 / pairs)

    def body(i, carry):
        cell = pl.multiple_of(i * step, step)
        for lane in range(0, D, 128):
            block(cell, lane)
        return carry

    lax.fori_loop(0, BLOCK // step, body, 0)

    total = jnp.sum(jnp.sum(wide[...], axis=0, keepdims=True), axis=1, keepdims=True)
    high = total.astype(BF16).astype(F32)
    middle = (total - high).astype(BF16).astype(F32)
    low = (total - high - middle).astype(BF16).astype(F32)
    lane_ids = lax.broadcasted_iota(jnp.int32, (4, 128), 1)
    at = jnp.where(lax.broadcasted_iota(jnp.int32, (4, 128), 0) == place[1], place[0], -128)
    spread = jnp.where(lane_ids == at, high, 0.0)
    spread = spread + jnp.where(lane_ids == at + REGIONS, middle, 0.0)
    spread = spread + jnp.where(lane_ids == at + 2 * REGIONS, low, 0.0)

    back = gst[...].reshape(CELLS, D)
    tn = (((0,), (0,)), ((), ()))
    d_out = lax.dot_general(shidden[...], back, tn, preferred_element_type=F32)
    pull = lax.dot_general(
        back, w_out[...], (((1,), (1,)), ((), ())), preferred_element_type=F32
    )
    gpre = (pull * slope[...]).astype(BF16)
    d_both = lax.dot_general(both[...], gpre, tn, preferred_element_type=F32)
    for half in range(2):
        for part in range(2):
            left = half * HALF + part * 128
            grads[half, :, 8 * part : 8 * part + 8] = d_both[:D, left : left + 128].reshape(
                TILES, 8, 128
            )
            grads[half, :, 16 + 8 * part : 24 + 8 * part] = d_out[:, left : left + 128].reshape(
                TILES, 8, 128
            )
            grads[half, :, 32 + 2 * part : 34 + 2 * part] = d_both[D:, left : left + 128].reshape(
                TILES, 2, 128
            )
        grads[half, :, LOSS_ROW : LOSS_ROW + 4] = jnp.broadcast_to(
            spread[None], (TILES, 4, 128)
        )


def halos(state):
    count = TILES
    ends = count - 1
    up = lax.ppermute(state[CELLS - HALO :], TILE, [(i, i + 1) for i in range(ends)])
    down = lax.ppermute(state[:HALO], TILE, [(i + 1, i) for i in range(ends)])
    return up, down


VMEM = pl.BlockSpec(memory_space=pltpu.VMEM)


def on_device(
    inputs,
    noise,
    neighbours,
    region_map,
    msg_weight,
    up_weight,
    down_weight,
    student_in,
    student_noise,
    student_out,
):
    state = inputs[0]
    both = jnp.concatenate([state, noise[0]], axis=1).reshape(MEMBERS, BLOCK, D + NOISE)
    top, bottom = halos(state)
    mine = lax.all_to_all(both, MEMBER, split_axis=0, concat_axis=0, tiled=True)
    teacher = pl.pallas_call(
        teacher_kernel,
        out_shape=jax.ShapeDtypeStruct((CELLS, D), BF16),
        in_specs=[VMEM] * 7,
        out_specs=VMEM,
        scratch_shapes=[pltpu.VMEM((CELLS + 2 * HALO, D), BF16)],
        name="teacher",
    )(top, state, bottom, neighbours, msg_weight, up_weight, down_weight)
    every = lax.all_to_all(
        teacher.reshape(MEMBERS, BLOCK, D), MEMBER, split_axis=0, concat_axis=0, tiled=True
    )
    mine = mine.reshape(CELLS, D + NOISE)
    student, shidden, slope = pl.pallas_call(
        student_kernel,
        out_shape=(
            jax.ShapeDtypeStruct((CELLS, D), BF16),
            jax.ShapeDtypeStruct((CELLS, H), BF16),
            jax.ShapeDtypeStruct((CELLS, H), F32),
        ),
        in_specs=[VMEM] * 4,
        out_specs=[VMEM] * 3,
        name="student",
    )(mine, student_in, student_noise, student_out)
    place = jnp.stack([region_map[0], lax.axis_index("core").astype(jnp.int32)])
    grads = pl.pallas_call(
        score_kernel,
        out_shape=jax.ShapeDtypeStruct((2, TILES, SHARE, 128), F32),
        in_specs=[VMEM] * 6 + [pl.BlockSpec(memory_space=pltpu.SMEM)],
        out_specs=VMEM,
        scratch_shapes=[
            pltpu.VMEM((MEMBERS, BLOCK, D), BF16),
            pltpu.VMEM((16, 128), F32),
        ],
        name="score",
    )(student.reshape(MEMBERS, BLOCK, D), every, mine, shidden, slope, student_out, place)
    own = lax.all_to_all(grads, "core", split_axis=0, concat_axis=0, tiled=True)
    half = jnp.sum(own, axis=0).astype(BF16)
    shares = lax.all_to_all(half, TILE, split_axis=0, concat_axis=0, tiled=True)
    share = jnp.sum(shares.astype(F32), axis=0)
    copies = jnp.broadcast_to(share[None], (MEMBERS, SHARE, 128))
    parts = lax.all_to_all(copies, MEMBER, split_axis=0, concat_axis=0, tiled=True)
    sums = jnp.sum(parts.reshape(MEMBERS // 2, 2, SHARE, 128), axis=0)

    def rows(first, count):
        piece = sums[:, first : first + 2 * count].reshape(2, 2, count, 128)
        return jnp.transpose(piece, (2, 0, 1, 3)).reshape(count, D)

    losses = sums[0, LOSS_ROW : LOSS_ROW + 2, : 3 * REGIONS].reshape(6, REGIONS)
    region_loss = jnp.sum(losses, axis=0) / (CELLS_ALL // REGIONS * D)
    return (teacher[None], region_loss, rows(0, 8), rows(32, 2), rows(16, 8))


def solution(mesh):
    split = Mesh(
        mesh.devices.reshape(4, 2, 2, 4, 8), ("member_0", "core", "tile_0", "tile_1", "tile_2")
    )
    in_specs = (
        P(MEMBER, TILE, None),
        P(MEMBER, TILE, None),
        P(None, TILE),
        P(TILE),
        P(),
        P(),
        P(),
        P(),
        P(),
        P(),
    )
    out_specs = (P(MEMBER, TILE, None), P(), P(TILE, None), P(TILE, None), P(TILE, None))
    return jax.shard_map(
        on_device, mesh=split, in_specs=in_specs, out_specs=out_specs, check_vma=False
    )
```

```python
import math

import jax
import jax.numpy as jnp
from jax import lax
from jax.experimental import pallas as pl
from jax.experimental.pallas import tpu as pltpu
from jax.sharding import Mesh
from jax.sharding import PartitionSpec as P

D = 512
FF = 1024
H = 512
NOISE = 128
NBRS = 8
HALO = 64
REGIONS = 8
MEMBERS = 8
CELLS = 512
BLOCK = CELLS // MEMBERS
CELLS_ALL = 32768
TILES = 64
HALF = D // 2
XY = TILES // 2
SHARE = 40
LOSS_ROW = 36

MEMBER = ("member_0", "core")
TILE = ("tile_0", "tile_1", "tile_2")
BF16 = jnp.bfloat16
F32 = jnp.float32


def teacher_kernel(top, state, bottom, near, msg, up, down, out, ext):
    ext[0:HALO] = top[...]
    ext[HALO : HALO + CELLS] = state[...]
    ext[HALO + CELLS :] = bottom[...]
    rows = 256
    sub = 128
    for at in range(0, CELLS, rows):
        parts = []
        for start in range(at, at + rows, sub):
            picks = near[:, start : start + sub].T
            lanes = lax.broadcasted_iota(jnp.int32, (sub, 2 * sub), 1) + start
            count = jnp.zeros((sub, 2 * sub), F32)
            for k in range(NBRS):
                count = count + jnp.where(picks[:, k : k + 1] == lanes, 1.0 / NBRS, 0.0)
            parts.append(
                jnp.dot(
                    count.astype(BF16),
                    ext[start : start + 2 * sub],
                    preferred_element_type=F32,
                ).astype(BF16)
            )
        gathered = jnp.concatenate(parts, axis=0)
        resid = state[at : at + rows].astype(F32) + jnp.dot(
            gathered, msg[...], preferred_element_type=F32
        )
        power = jnp.mean(resid * resid, axis=1, keepdims=True)
        normed = (resid * lax.rsqrt(power + 1e-06)).astype(BF16)
        hidden = jax.nn.silu(jnp.dot(normed, up[...], preferred_element_type=F32)).astype(BF16)
        out[at : at + rows] = (
            resid + jnp.dot(hidden, down[...], preferred_element_type=F32)
        ).astype(BF16)


def join_kernel(state, noise, both, sem):
    copies = [
        pltpu.make_async_copy(state, both.at[:, :D], sem.at[0]),
        pltpu.make_async_copy(noise, both.at[:, D:], sem.at[1]),
    ]
    for copy in copies:
        copy.start()
    for copy in copies:
        copy.wait()


def student_kernel(mine, w_in, w_noise, w_out, student, shidden, slope, turned):
    rows = 256
    for at in range(0, CELLS, rows):
        state = mine[at : at + rows, :D]
        preact = jnp.dot(state, w_in[...], preferred_element_type=F32) + jnp.dot(
            mine[at : at + rows, D:], w_noise[...], preferred_element_type=F32
        )
        sig = jax.nn.sigmoid(preact)
        hid = (preact * sig).astype(BF16)
        slope[at : at + rows] = sig * (1.0 + preact * (1.0 - sig))
        student[at : at + rows] = (
            state.astype(F32) + jnp.dot(hid, w_out[...], preferred_element_type=F32)
        ).astype(BF16)
        shidden[:, at : at + rows] = hid.T
        turned[:, at : at + rows] = mine[at : at + rows].T


def score_kernel(
    student,
    teacher,
    turned_at,
    shidden_at,
    slope_at,
    w_out_at,
    place,
    send,
    keep,
    gst,
    gpre,
    wide,
    turned,
    shidden,
    slope,
    w_out,
    sem,
):
    copies = [
        pltpu.make_async_copy(source, target, sem.at[k])
        for k, (source, target) in enumerate(
            ((turned_at, turned), (shidden_at, shidden), (slope_at, slope), (w_out_at, w_out))
        )
    ]
    for copy in copies:
        copy.start()
    step = 16
    wide[...] = jnp.zeros_like(wide)

    def block(cell, lane):
        s = [student[m, pl.ds(cell, step), lane : lane + 128].astype(F32) for m in range(MEMBERS)]
        g = [jnp.zeros((step, 128), F32) for _ in range(MEMBERS)]
        loss = jnp.zeros((step, 128), F32)
        for n in range(MEMBERS):
            t = teacher[n, pl.ds(cell, step), lane : lane + 128].astype(F32)
            for m in range(MEMBERS):
                d = s[m] - t
                q = d * d + 0.01
                inv = lax.rsqrt(q)
                loss = loss + q * inv
                g[m] = g[m] + d * inv
        ratio = (MEMBERS - 1) / MEMBERS
        loss = loss * ratio
        g = [x * ratio for x in g]
        for m in range(MEMBERS):
            for n in range(m + 1, MEMBERS):
                d = s[m] - s[n]
                q = d * d + 0.01
                inv = lax.rsqrt(q)
                r = d * inv
                loss = loss - q * inv
                g[m] = g[m] - r
                g[n] = g[n] + r
        scale = 1.0 / (MEMBERS * (MEMBERS - 1) * math.sqrt(CELLS_ALL))
        for m in range(MEMBERS):
            gst[m, pl.ds(cell, step), lane : lane + 128] = (g[m] * scale).astype(BF16)
        pairs = MEMBERS * (MEMBERS - 1)
        wide[...] += (loss - 0.1 * (pairs - pairs // 2)) * (1.0 / pairs)

    def body(i, carry):
        cell = pl.multiple_of(i * step, step)
        for lane in range(0, D, 128):
            block(cell, lane)
        return carry

    lax.fori_loop(0, BLOCK // step, body, 0)

    total = jnp.sum(jnp.sum(wide[...], axis=0, keepdims=True), axis=1, keepdims=True)
    lane_ids = lax.broadcasted_iota(jnp.int32, (4, 128), 1)
    at = jnp.where(lax.broadcasted_iota(jnp.int32, (4, 128), 0) == place[1], place[0], -128)
    spread = jnp.zeros((4, 128), F32)
    for k, piece in enumerate(three(total)):
        spread = spread + jnp.where(lane_ids == at + k * REGIONS, piece, 0.0)
    spread = jnp.broadcast_to(spread[None], (XY, 4, 128))

    for copy in copies:
        copy.wait()
    back = gst[...].reshape(CELLS, D)
    pull = lax.dot_general(
        back, w_out[...], (((1,), (1,)), ((), ())), preferred_element_type=F32
    )
    gpre[...] = (pull * slope[...]).astype(BF16)
    for k, target in enumerate((send, keep)):
        left = pl.multiple_of(jnp.where(place[1] == k, HALF, 0), HALF)
        d_out = jnp.dot(
            shidden[...], gst[:, :, pl.ds(left, HALF)].reshape(CELLS, HALF), preferred_element_type=F32
        )
        pulled = gpre[:, pl.ds(left, HALF)]
        d_in = jnp.dot(turned[:D], pulled, preferred_element_type=F32)
        d_noise = jnp.dot(turned[D:], pulled, preferred_element_type=F32)
        for high in range(2):
            pieces = []
            for source, count in ((d_in, 8), (d_out, 8), (d_noise, 2)):
                start = high * XY * count
                for lane in (0, 128):
                    pieces.append(
                        source[start : start + XY * count, lane : lane + 128].reshape(
                            XY, count, 128
                        )
                    )
            pieces.append(spread)
            target[:, high] = jnp.concatenate(pieces, axis=1).astype(BF16)


def three(value):
    high = value.astype(BF16).astype(F32)
    middle = (value - high).astype(BF16).astype(F32)
    return high, middle, (value - high - middle).astype(BF16).astype(F32)


def fold_kernel(arrived, out):
    lanes = lax.broadcasted_iota(jnp.int32, (4, 128), 1)
    first = lax.broadcasted_iota(jnp.int32, (4, 128), 0) == 0
    for high in range(2):
        total = jnp.zeros((SHARE, 128), F32)
        for k in range(XY):
            total = total + arrived[k, high].astype(F32)
        tail = total[LOSS_ROW:]
        row = jnp.sum(tail, axis=0, keepdims=True)
        loss = row[:, :REGIONS] + row[:, REGIONS : 2 * REGIONS] + row[:, 2 * REGIONS : 3 * REGIONS]
        again = jnp.concatenate(
            [*three(loss), jnp.zeros((1, 128 - 3 * REGIONS), F32)], axis=1
        )
        share = jnp.concatenate(
            [total[:LOSS_ROW], jnp.where(first, again, jnp.zeros_like(tail))], axis=0
        ).astype(BF16)
        for k in range(MEMBERS):
            out[high * MEMBERS + k] = share


def last_kernel(arrived, region_loss, grad_in, grad_noise, grad_out):
    for half in range(2):
        total = arrived[half].astype(F32)
        for k in range(1, MEMBERS):
            total = total + arrived[2 * k + half].astype(F32)
        for part in range(2):
            left = half * HALF + part * 128
            grad_in[:, left : left + 128] = total[8 * part : 8 * part + 8]
            grad_out[:, left : left + 128] = total[16 + 8 * part : 24 + 8 * part]
            grad_noise[:, left : left + 128] = total[32 + 2 * part : 34 + 2 * part]
        if half == 0:
            row = total[LOSS_ROW : LOSS_ROW + 1]
            loss = (
                row[:, :REGIONS]
                + row[:, REGIONS : 2 * REGIONS]
                + row[:, 2 * REGIONS : 3 * REGIONS]
            )
            region_loss[...] = loss * (1.0 / (CELLS_ALL // REGIONS * D))


def halos(state):
    count = TILES
    ends = count - 1
    up = lax.ppermute(state[CELLS - HALO :], TILE, [(i, i + 1) for i in range(ends)])
    down = lax.ppermute(state[:HALO], TILE, [(i + 1, i) for i in range(ends)])
    return up, down


HBM = pl.BlockSpec(memory_space=pltpu.HBM)
VMEM = pl.BlockSpec(memory_space=pltpu.VMEM)
PARAMS = pltpu.CompilerParams(vmem_limit_bytes=16 * 1024 * 1024)


def in_hbm(array):
    return pltpu.with_memory_space_constraint(array, pltpu.HBM)


def on_device(
    inputs,
    noise,
    neighbours,
    region_map,
    msg_weight,
    up_weight,
    down_weight,
    student_in,
    student_noise,
    student_out,
):
    state = inputs[0]
    with jax.named_scope("rows"):
        both = pl.pallas_call(
            join_kernel,
            out_shape=jax.ShapeDtypeStruct((CELLS, D + NOISE), BF16),
            in_specs=[HBM] * 2,
            out_specs=HBM,
            scratch_shapes=[pltpu.SemaphoreType.DMA((2,))],
            compiler_params=PARAMS,
            name="join",
        )(in_hbm(state), in_hbm(noise[0]))
        mine = lax.all_to_all(
            both.reshape(MEMBERS, BLOCK, D + NOISE),
            MEMBER,
            split_axis=0,
            concat_axis=0,
            tiled=True,
        )
    with jax.named_scope("halo"):
        top, bottom = halos(state)
    teach = pl.pallas_call(
        teacher_kernel,
        out_shape=jax.ShapeDtypeStruct((CELLS, D), BF16),
        in_specs=[VMEM] * 7,
        out_specs=VMEM,
        scratch_shapes=[pltpu.VMEM((CELLS + 2 * HALO, D), BF16)],
        compiler_params=PARAMS,
        name="teacher",
    )
    with jax.named_scope("teach"):
        teacher = teach(top, state, bottom, neighbours, msg_weight, up_weight, down_weight)
    with jax.named_scope("every"):
        every = lax.all_to_all(
            teacher.reshape(MEMBERS, BLOCK, D), MEMBER, split_axis=0, concat_axis=0, tiled=True
        )
    mine = mine.reshape(CELLS, D + NOISE)
    pupil = pl.pallas_call(
        student_kernel,
        out_shape=(
            jax.ShapeDtypeStruct((CELLS, D), BF16),
            jax.ShapeDtypeStruct((H, CELLS), BF16),
            jax.ShapeDtypeStruct((CELLS, H), F32),
            jax.ShapeDtypeStruct((D + NOISE, CELLS), BF16),
        ),
        in_specs=[VMEM] * 4,
        out_specs=[VMEM] * 4,
        compiler_params=PARAMS,
        name="student",
    )
    with jax.named_scope("pupil"):
        student, shidden, slope, turned = pupil(mine, student_in, student_noise, student_out)
    place = jnp.stack([region_map[0], lax.axis_index("core").astype(jnp.int32)])
    send, keep = pl.pallas_call(
        score_kernel,
        out_shape=[jax.ShapeDtypeStruct((XY, 2, SHARE, 128), BF16)] * 2,
        in_specs=[VMEM] * 2 + [HBM] * 4 + [pl.BlockSpec(memory_space=pltpu.SMEM)],
        out_specs=[VMEM] * 2,
        scratch_shapes=[
            pltpu.VMEM((MEMBERS, BLOCK, D), BF16),
            pltpu.VMEM((CELLS, D), BF16),
            pltpu.VMEM((16, 128), F32),
            pltpu.VMEM((D + NOISE, CELLS), BF16),
            pltpu.VMEM((H, CELLS), BF16),
            pltpu.VMEM((CELLS, H), F32),
            pltpu.VMEM((H, D), BF16),
            pltpu.SemaphoreType.DMA((4,)),
        ],
        compiler_params=PARAMS,
        name="score",
    )(
        student.reshape(MEMBERS, BLOCK, D),
        every,
        in_hbm(turned),
        in_hbm(shidden),
        in_hbm(slope),
        in_hbm(student_out),
        place,
    )
    other = lax.ppermute(send, "core", [(0, 1), (1, 0)])
    half = (keep.astype(F32) + other.astype(F32)).astype(BF16)
    shares = lax.all_to_all(half, ("tile_1", "tile_2"), split_axis=0, concat_axis=0, tiled=True)
    copies = pl.pallas_call(
        fold_kernel,
        out_shape=jax.ShapeDtypeStruct((2 * MEMBERS, SHARE, 128), BF16),
        in_specs=[VMEM],
        out_specs=VMEM,
        compiler_params=PARAMS,
        name="fold",
    )(shares)
    parts = lax.all_to_all(
        copies, ("tile_0", "member_0", "core"), split_axis=0, concat_axis=0, tiled=True
    )
    region_loss, grad_in, grad_noise, grad_out = pl.pallas_call(
        last_kernel,
        out_shape=[
            jax.ShapeDtypeStruct((1, REGIONS), F32),
            jax.ShapeDtypeStruct((8, D), F32),
            jax.ShapeDtypeStruct((2, D), F32),
            jax.ShapeDtypeStruct((8, D), F32),
        ],
        in_specs=[VMEM],
        out_specs=[VMEM] * 4,
        compiler_params=PARAMS,
        name="last",
    )(parts)
    return (teacher[None], region_loss.reshape(REGIONS), grad_in, grad_noise, grad_out)


def solution(mesh):
    split = Mesh(
        mesh.devices.reshape(4, 2, 2, 4, 8), ("member_0", "core", "tile_0", "tile_1", "tile_2")
    )
    in_specs = (
        P(MEMBER, TILE, None),
        P(MEMBER, TILE, None),
        P(None, TILE),
        P(TILE),
        P(),
        P(),
        P(),
        P(),
        P(),
        P(),
    )
    out_specs = (P(MEMBER, TILE, None), P(), P(TILE, None), P(TILE, None), P(TILE, None))
    return jax.shard_map(
        on_device, mesh=split, in_specs=in_specs, out_specs=out_specs, check_vma=False
    )
```

```python
import math

import jax
import jax.numpy as jnp
from jax import lax
from jax.experimental import pallas as pl
from jax.experimental.pallas import tpu as pltpu
from jax.sharding import Mesh
from jax.sharding import PartitionSpec as P

D = 512
H = 512
NOISE = 128
NBRS = 8
HALO = 64
REGIONS = 8
MEMBERS = 8
CELLS = 512
BLOCK = CELLS // MEMBERS
CELLS_ALL = 32768
TILES = 64
HALF = D // 2
XY = TILES // 2
SHARE = 40
LOSS_ROW = 36

MEMBER = ("member_0", "core")
TILE = ("tile_0", "tile_1", "tile_2")
BF16 = jnp.bfloat16
F32 = jnp.float32


def teacher_kernel(
    top, top_far, state, bottom, bottom_far, near, msg_at, up, down, out, ext, msg, sem
):
    copy = pltpu.make_async_copy(msg_at, msg, sem)
    copy.start()
    ext[0:HALO] = top[...] + top_far[...]
    ext[HALO : HALO + CELLS] = state[...]
    ext[HALO + CELLS :] = bottom[...] + bottom_far[...]
    rows = 256
    sub = 128
    for at in range(0, CELLS, rows):
        parts = []
        for start in range(at, at + rows, sub):
            picks = near[:, start : start + sub].T
            lanes = lax.broadcasted_iota(jnp.int32, (sub, 2 * sub), 1) + start
            count = jnp.zeros((sub, 2 * sub), F32)
            for k in range(NBRS):
                count = count + jnp.where(picks[:, k : k + 1] == lanes, 1.0 / NBRS, 0.0)
            parts.append(
                jnp.dot(
                    count.astype(BF16),
                    ext[start : start + 2 * sub],
                    preferred_element_type=F32,
                ).astype(BF16)
            )
        gathered = jnp.concatenate(parts, axis=0)
        if at == 0:
            copy.wait()
        resid = state[at : at + rows].astype(F32) + jnp.dot(
            gathered, msg[...], preferred_element_type=F32
        )
        power = jnp.mean(resid * resid, axis=1, keepdims=True)
        normed = (resid * lax.rsqrt(power + 1e-06)).astype(BF16)
        hidden = jax.nn.silu(jnp.dot(normed, up[...], preferred_element_type=F32)).astype(BF16)
        out[at : at + rows] = (
            resid + jnp.dot(hidden, down[...], preferred_element_type=F32)
        ).astype(BF16)


def join_kernel(state, noise, both, sem):
    copies = [
        pltpu.make_async_copy(state, both.at[:, :D], sem.at[0]),
        pltpu.make_async_copy(noise, both.at[:, D:], sem.at[1]),
    ]
    for copy in copies:
        copy.start()
    for copy in copies:
        copy.wait()


def student_kernel(mine, w_in, w_noise, w_out, student, shidden, slope, turned):
    rows = 256
    for at in range(0, CELLS, rows):
        state = mine[at : at + rows, :D]
        preact = jnp.dot(state, w_in[...], preferred_element_type=F32) + jnp.dot(
            mine[at : at + rows, D:], w_noise[...], preferred_element_type=F32
        )
        sig = jax.nn.sigmoid(preact)
        hid = (preact * sig).astype(BF16)
        slope[at : at + rows] = sig * (1.0 + preact * (1.0 - sig))
        student[at : at + rows] = (
            state.astype(F32) + jnp.dot(hid, w_out[...], preferred_element_type=F32)
        ).astype(BF16)
        shidden[:, at : at + rows] = hid.T
        turned[:, at : at + rows] = mine[at : at + rows].T


def score_kernel(
    student,
    teacher,
    turned_at,
    shidden_at,
    slope_at,
    w_out_at,
    place,
    send,
    keep,
    gst,
    gpre,
    wide,
    turned,
    shidden,
    slope,
    w_out,
    sem,
):
    copies = [
        pltpu.make_async_copy(source, target, sem.at[k])
        for k, (source, target) in enumerate(
            ((turned_at, turned), (shidden_at, shidden), (slope_at, slope), (w_out_at, w_out))
        )
    ]
    for copy in copies:
        copy.start()
    step = 16
    wide[...] = jnp.zeros_like(wide)

    def block(cell, lane):
        s = [student[m, pl.ds(cell, step), lane : lane + 128].astype(F32) for m in range(MEMBERS)]
        g = [jnp.zeros((step, 128), F32) for _ in range(MEMBERS)]
        loss = jnp.zeros((step, 128), F32)
        for n in range(MEMBERS):
            t = teacher[n, pl.ds(cell, step), lane : lane + 128].astype(F32)
            for m in range(MEMBERS):
                d = s[m] - t
                q = d * d + 0.01
                inv = lax.rsqrt(q)
                loss = loss + q * inv
                g[m] = g[m] + d * inv
        ratio = (MEMBERS - 1) / MEMBERS
        loss = loss * ratio
        g = [x * ratio for x in g]
        for m in range(MEMBERS):
            for n in range(m + 1, MEMBERS):
                d = s[m] - s[n]
                q = d * d + 0.01
                inv = lax.rsqrt(q)
                r = d * inv
                loss = loss - q * inv
                g[m] = g[m] - r
                g[n] = g[n] + r
        scale = 1.0 / (MEMBERS * (MEMBERS - 1) * math.sqrt(CELLS_ALL))
        for m in range(MEMBERS):
            gst[m, pl.ds(cell, step), lane : lane + 128] = (g[m] * scale).astype(BF16)
        pairs = MEMBERS * (MEMBERS - 1)
        wide[...] += (loss - 0.1 * (pairs - pairs // 2)) * (1.0 / pairs)

    def body(i, carry):
        cell = pl.multiple_of(i * step, step)
        for lane in range(0, D, 128):
            block(cell, lane)
        return carry

    lax.fori_loop(0, BLOCK // step, body, 0)

    total = jnp.sum(jnp.sum(wide[...], axis=0, keepdims=True), axis=1, keepdims=True)
    lane_ids = lax.broadcasted_iota(jnp.int32, (4, 128), 1)
    at = jnp.where(lax.broadcasted_iota(jnp.int32, (4, 128), 0) == place[1], place[0], -128)
    spread = jnp.zeros((4, 128), F32)
    for k, piece in enumerate(three(total)):
        spread = spread + jnp.where(lane_ids == at + k * REGIONS, piece, 0.0)
    spread = jnp.broadcast_to(spread[None], (XY, 4, 128))

    for copy in copies:
        copy.wait()
    back = gst[...].reshape(CELLS, D)
    pull = lax.dot_general(
        back, w_out[...], (((1,), (1,)), ((), ())), preferred_element_type=F32
    )
    gpre[...] = (pull * slope[...]).astype(BF16)
    for k, target in enumerate((send, keep)):
        left = pl.multiple_of(jnp.where(place[1] == k, HALF, 0), HALF)
        d_out = jnp.dot(
            shidden[...], gst[:, :, pl.ds(left, HALF)].reshape(CELLS, HALF), preferred_element_type=F32
        )
        pulled = gpre[:, pl.ds(left, HALF)]
        d_in = jnp.dot(turned[:D], pulled, preferred_element_type=F32)
        d_noise = jnp.dot(turned[D:], pulled, preferred_element_type=F32)
        for high in range(2):
            pieces = []
            for source, count in ((d_in, 8), (d_out, 8), (d_noise, 2)):
                start = high * XY * count
                for lane in (0, 128):
                    pieces.append(
                        source[start : start + XY * count, lane : lane + 128].reshape(
                            XY, count, 128
                        )
                    )
            pieces.append(spread)
            target[:, high] = jnp.concatenate(pieces, axis=1).astype(BF16)


def three(value):
    high = value.astype(BF16).astype(F32)
    middle = (value - high).astype(BF16).astype(F32)
    return high, middle, (value - high - middle).astype(BF16).astype(F32)


def fold_kernel(arrived, out):
    lanes = lax.broadcasted_iota(jnp.int32, (4, 128), 1)
    first = lax.broadcasted_iota(jnp.int32, (4, 128), 0) == 0
    for high in range(2):
        total = jnp.zeros((SHARE, 128), F32)
        for k in range(XY):
            total = total + arrived[k, high].astype(F32)
        tail = total[LOSS_ROW:]
        row = jnp.sum(tail, axis=0, keepdims=True)
        loss = row[:, :REGIONS] + row[:, REGIONS : 2 * REGIONS] + row[:, 2 * REGIONS : 3 * REGIONS]
        again = jnp.concatenate(
            [*three(loss), jnp.zeros((1, 128 - 3 * REGIONS), F32)], axis=1
        )
        share = jnp.concatenate(
            [total[:LOSS_ROW], jnp.where(first, again, jnp.zeros_like(tail))], axis=0
        ).astype(BF16)
        for k in range(MEMBERS):
            out[high * MEMBERS + k] = share


def last_kernel(arrived, region_loss, grad_in, grad_noise, grad_out):
    for half in range(2):
        total = arrived[half].astype(F32)
        for k in range(1, MEMBERS):
            total = total + arrived[2 * k + half].astype(F32)
        for part in range(2):
            left = half * HALF + part * 128
            grad_in[:, left : left + 128] = total[8 * part : 8 * part + 8]
            grad_out[:, left : left + 128] = total[16 + 8 * part : 24 + 8 * part]
            grad_noise[:, left : left + 128] = total[32 + 2 * part : 34 + 2 * part]
        if half == 0:
            row = total[LOSS_ROW : LOSS_ROW + 1]
            loss = (
                row[:, :REGIONS]
                + row[:, REGIONS : 2 * REGIONS]
                + row[:, 2 * REGIONS : 3 * REGIONS]
            )
            region_loss[...] = loss * (1.0 / (CELLS_ALL // REGIONS * D))


def halos(state, links):
    up = lax.ppermute(state[CELLS - HALO :], TILE, [(i, i + 1) for i in links])
    down = lax.ppermute(state[:HALO], TILE, [(i + 1, i) for i in links])
    return up, down


HBM = pl.BlockSpec(memory_space=pltpu.HBM)
VMEM = pl.BlockSpec(memory_space=pltpu.VMEM)
PARAMS = pltpu.CompilerParams(vmem_limit_bytes=16 * 1024 * 1024)


def in_hbm(array):
    return pltpu.with_memory_space_constraint(array, pltpu.HBM)


def step(
    inputs,
    noise,
    neighbours,
    region_map,
    msg_weight,
    up_weight,
    down_weight,
    student_in,
    student_noise,
    student_out,
):
    state = inputs[0]
    both = pl.pallas_call(
        join_kernel,
        out_shape=jax.ShapeDtypeStruct((CELLS, D + NOISE), BF16),
        in_specs=[HBM] * 2,
        out_specs=VMEM,
        scratch_shapes=[pltpu.SemaphoreType.DMA((2,))],
        compiler_params=PARAMS,
        name="join",
    )(in_hbm(state), in_hbm(noise[0]))
    mine = lax.all_to_all(
        both.reshape(MEMBERS, BLOCK, D + NOISE),
        MEMBER,
        split_axis=0,
        concat_axis=0,
        tiled=True,
    )
    top_far, bottom_far = halos(state, [XY - 1])
    top, bottom = halos(state, [i for i in range(TILES - 1) if i != XY - 1])
    teach = pl.pallas_call(
        teacher_kernel,
        out_shape=jax.ShapeDtypeStruct((CELLS, D), BF16),
        in_specs=[VMEM] * 6 + [HBM] + [VMEM] * 2,
        out_specs=VMEM,
        scratch_shapes=[
            pltpu.VMEM((CELLS + 2 * HALO, D), BF16),
            pltpu.VMEM((D, D), BF16),
            pltpu.SemaphoreType.DMA,
        ],
        compiler_params=PARAMS,
        name="teacher",
    )
    teacher = teach(
        top,
        top_far,
        state,
        bottom,
        bottom_far,
        neighbours,
        in_hbm(msg_weight),
        up_weight,
        down_weight,
    )
    every = lax.all_to_all(
        teacher.reshape(MEMBERS, BLOCK, D), MEMBER, split_axis=0, concat_axis=0, tiled=True
    )
    mine = mine.reshape(CELLS, D + NOISE)
    pupil = pl.pallas_call(
        student_kernel,
        out_shape=(
            jax.ShapeDtypeStruct((CELLS, D), BF16),
            jax.ShapeDtypeStruct((H, CELLS), BF16),
            jax.ShapeDtypeStruct((CELLS, H), F32),
            jax.ShapeDtypeStruct((D + NOISE, CELLS), BF16),
        ),
        in_specs=[VMEM] * 4,
        out_specs=[VMEM] * 4,
        compiler_params=PARAMS,
        name="student",
    )
    student, shidden, slope, turned = pupil(mine, student_in, student_noise, student_out)
    place = jnp.stack([region_map[0], lax.axis_index("core").astype(jnp.int32)])
    send, keep = pl.pallas_call(
        score_kernel,
        out_shape=[jax.ShapeDtypeStruct((XY, 2, SHARE, 128), BF16)] * 2,
        in_specs=[VMEM] * 2 + [HBM] * 4 + [pl.BlockSpec(memory_space=pltpu.SMEM)],
        out_specs=[VMEM] * 2,
        scratch_shapes=[
            pltpu.VMEM((MEMBERS, BLOCK, D), BF16),
            pltpu.VMEM((CELLS, D), BF16),
            pltpu.VMEM((16, 128), F32),
            pltpu.VMEM((D + NOISE, CELLS), BF16),
            pltpu.VMEM((H, CELLS), BF16),
            pltpu.VMEM((CELLS, H), F32),
            pltpu.VMEM((H, D), BF16),
            pltpu.SemaphoreType.DMA((4,)),
        ],
        compiler_params=PARAMS,
        name="score",
    )(
        student.reshape(MEMBERS, BLOCK, D),
        every,
        in_hbm(turned),
        in_hbm(shidden),
        in_hbm(slope),
        in_hbm(student_out),
        place,
    )
    other = lax.ppermute(send, "core", [(0, 1), (1, 0)])
    half = (keep.astype(F32) + other.astype(F32)).astype(BF16)
    shares = lax.all_to_all(half, ("tile_1", "tile_2"), split_axis=0, concat_axis=0, tiled=True)
    copies = pl.pallas_call(
        fold_kernel,
        out_shape=jax.ShapeDtypeStruct((2 * MEMBERS, SHARE, 128), BF16),
        in_specs=[VMEM],
        out_specs=VMEM,
        compiler_params=PARAMS,
        name="fold",
    )(shares)
    parts = lax.all_to_all(
        copies, ("tile_0", "member_0", "core"), split_axis=0, concat_axis=0, tiled=True
    )
    region_loss, grad_in, grad_noise, grad_out = pl.pallas_call(
        last_kernel,
        out_shape=[
            jax.ShapeDtypeStruct((1, REGIONS), F32),
            jax.ShapeDtypeStruct((8, D), F32),
            jax.ShapeDtypeStruct((2, D), F32),
            jax.ShapeDtypeStruct((8, D), F32),
        ],
        in_specs=[VMEM],
        out_specs=[VMEM] * 4,
        compiler_params=PARAMS,
        name="last",
    )(parts)
    return (teacher[None], region_loss.reshape(REGIONS), grad_in, grad_noise, grad_out)


def solution(mesh):
    split = Mesh(
        mesh.devices.reshape(4, 2, 2, 4, 8), ("member_0", "core", "tile_0", "tile_1", "tile_2")
    )
    in_specs = (
        P(MEMBER, TILE, None),
        P(MEMBER, TILE, None),
        P(None, TILE),
        P(TILE),
        P(),
        P(),
        P(),
        P(),
        P(),
        P(),
    )
    out_specs = (P(MEMBER, TILE, None), P(), P(TILE, None), P(TILE, None), P(TILE, None))
    return jax.shard_map(step, mesh=split, in_specs=in_specs, out_specs=out_specs, check_vma=False)
```

```python
import math

import jax
import jax.numpy as jnp
from jax import lax
from jax.experimental import pallas as pl
from jax.experimental.pallas import tpu as pltpu
from jax.sharding import Mesh
from jax.sharding import PartitionSpec as P

D = 512
H = 512
NOISE = 128
NBRS = 8
HALO = 64
REGIONS = 8
MEMBERS = 8
CELLS = 512
BLOCK = CELLS // MEMBERS
CELLS_ALL = 32768
TILES = 64
HALF = D // 2
XY = TILES // 2
JOINS = 4
SHARE = 40
LOSS_ROW = 36

MEMBER = ("member_0", "core")
TILE = ("tile_0", "tile_1", "tile_2")
BF16 = jnp.bfloat16
F32 = jnp.float32


def counts(picks, start, rows, width):
    lanes = lax.broadcasted_iota(jnp.int32, (rows, width), 1) + start
    count = jnp.zeros((rows, width), F32)
    for k in range(NBRS):
        count = count + jnp.where(picks[:, k : k + 1] == lanes, 1.0 / NBRS, 0.0)
    return count.astype(BF16)


def teach(state, gathered, msg, up, down):
    resid = state.astype(F32) + jnp.dot(gathered, msg, preferred_element_type=F32)
    power = jnp.mean(resid * resid, axis=1, keepdims=True)
    normed = (resid * lax.rsqrt(power + 1e-06)).astype(BF16)
    hidden = jax.nn.silu(jnp.dot(normed, up, preferred_element_type=F32)).astype(BF16)
    return (resid + jnp.dot(hidden, down, preferred_element_type=F32)).astype(BF16)


def middle_kernel(state, near, msg_at, up, down, out, msg, held, sem, out_sem):
    copy = pltpu.make_async_copy(msg_at, msg, sem)
    copy.start()
    sub = 128
    parts = []
    for at in range(0, CELLS - 2 * HALO, sub):
        picks = near[:, HALO + at : HALO + at + sub].T
        parts.append(
            jnp.dot(
                counts(picks, HALO + at, sub, 2 * sub),
                state[at : at + 2 * sub],
                preferred_element_type=F32,
            ).astype(BF16)
        )
    copy.wait()
    half = (CELLS - 2 * HALO) // 2
    gathered = jnp.concatenate(parts, axis=0)
    writes = []
    for k, at in enumerate((0, half)):
        held[at : at + half] = teach(
            state[HALO + at : HALO + at + half],
            gathered[at : at + half],
            msg[...],
            up[...],
            down[...],
        )
        writes.append(
            pltpu.make_async_copy(
                held.at[at : at + half], out.at[HALO + at : HALO + at + half], out_sem.at[k]
            )
        )
        writes[-1].start()
    for copy in writes:
        copy.wait()


def edges_kernel(top, top_far, state, bottom, bottom_far, near, msg, up, down, partly, out, held, sem):
    reach = 3 * HALO
    above = jnp.concatenate([top[...] + top_far[...], state[: 2 * HALO]], axis=0)
    below = jnp.concatenate([state[CELLS - 2 * HALO :], bottom[...] + bottom_far[...]], axis=0)
    first = near[:, : 2 * HALO].T[:HALO]
    last = near[:, CELLS - 2 * HALO :].T[HALO:]
    gathered = jnp.concatenate(
        [
            jnp.dot(counts(first, 0, HALO, reach), above, preferred_element_type=F32),
            jnp.dot(
                counts(last, CELLS - HALO, HALO, reach), below, preferred_element_type=F32
            ),
        ],
        axis=0,
    ).astype(BF16)
    ends = jnp.concatenate([state[:HALO], state[CELLS - HALO :]], axis=0)
    held[...] = teach(ends, gathered, msg[...], up[...], down[...])
    writes = [
        pltpu.make_async_copy(held.at[:HALO], out.at[:HALO], sem.at[0]),
        pltpu.make_async_copy(held.at[HALO:], out.at[CELLS - HALO :], sem.at[1]),
    ]
    for copy in writes:
        copy.start()
    for copy in writes:
        copy.wait()


def join_kernel(state, noise, both, held, sem, out_sem):
    rows = CELLS // JOINS
    reads = []
    for k in range(JOINS):
        at = pl.ds(k * rows, rows)
        reads.append(
            (
                pltpu.make_async_copy(state.at[at], held.at[at, :D], sem.at[2 * k]),
                pltpu.make_async_copy(noise.at[at], held.at[at, D:], sem.at[2 * k + 1]),
            )
        )
        for copy in reads[-1]:
            copy.start()
    writes = []
    for k in range(JOINS):
        at = pl.ds(k * rows, rows)
        for copy in reads[k]:
            copy.wait()
        writes.append(pltpu.make_async_copy(held.at[at], both.at[at], out_sem.at[k]))
        writes[-1].start()
    for copy in writes:
        copy.wait()


def student_kernel(mine, w_in, w_noise, w_out, student, shidden, slope, turned):
    rows = 256
    for at in range(0, CELLS, rows):
        state = mine[at : at + rows, :D]
        preact = jnp.dot(state, w_in[...], preferred_element_type=F32) + jnp.dot(
            mine[at : at + rows, D:], w_noise[...], preferred_element_type=F32
        )
        sig = jax.nn.sigmoid(preact)
        hid = (preact * sig).astype(BF16)
        slope[at : at + rows] = sig * (1.0 + preact * (1.0 - sig))
        student[at : at + rows] = (
            state.astype(F32) + jnp.dot(hid, w_out[...], preferred_element_type=F32)
        ).astype(BF16)
        shidden[:, at : at + rows] = hid.T
        turned[:, at : at + rows] = mine[at : at + rows].T


def score_kernel(
    student,
    teacher,
    turned_at,
    shidden_at,
    slope_at,
    w_out_at,
    place,
    send,
    keep,
    gst,
    gpre,
    wide,
    turned,
    shidden,
    slope,
    w_out,
    sem,
):
    copies = [
        pltpu.make_async_copy(source, target, sem.at[k])
        for k, (source, target) in enumerate(
            ((turned_at, turned), (shidden_at, shidden), (slope_at, slope), (w_out_at, w_out))
        )
    ]
    for copy in copies:
        copy.start()
    step = 16
    wide[...] = jnp.zeros_like(wide)

    def block(cell, lane):
        s = [student[m, pl.ds(cell, step), lane : lane + 128].astype(F32) for m in range(MEMBERS)]
        g = [jnp.zeros((step, 128), F32) for _ in range(MEMBERS)]
        loss = jnp.zeros((step, 128), F32)
        for n in range(MEMBERS):
            t = teacher[n, pl.ds(cell, step), lane : lane + 128].astype(F32)
            for m in range(MEMBERS):
                d = s[m] - t
                q = d * d + 0.01
                inv = lax.rsqrt(q)
                loss = loss + q * inv
                g[m] = g[m] + d * inv
        ratio = (MEMBERS - 1) / MEMBERS
        loss = loss * ratio
        g = [x * ratio for x in g]
        for m in range(MEMBERS):
            for n in range(m + 1, MEMBERS):
                d = s[m] - s[n]
                q = d * d + 0.01
                inv = lax.rsqrt(q)
                r = d * inv
                loss = loss - q * inv
                g[m] = g[m] - r
                g[n] = g[n] + r
        scale = 1.0 / (MEMBERS * (MEMBERS - 1) * math.sqrt(CELLS_ALL))
        for m in range(MEMBERS):
            gst[m, pl.ds(cell, step), lane : lane + 128] = (g[m] * scale).astype(BF16)
        pairs = MEMBERS * (MEMBERS - 1)
        wide[...] += (loss - 0.1 * (pairs - pairs // 2)) * (1.0 / pairs)

    def body(i, carry):
        cell = pl.multiple_of(i * step, step)
        for lane in range(0, D, 128):
            block(cell, lane)
        return carry

    lax.fori_loop(0, BLOCK // step, body, 0)

    total = jnp.sum(jnp.sum(wide[...], axis=0, keepdims=True), axis=1, keepdims=True)
    lane_ids = lax.broadcasted_iota(jnp.int32, (4, 128), 1)
    at = jnp.where(lax.broadcasted_iota(jnp.int32, (4, 128), 0) == place[1], place[0], -128)
    spread = jnp.zeros((4, 128), F32)
    for k, piece in enumerate(three(total)):
        spread = spread + jnp.where(lane_ids == at + k * REGIONS, piece, 0.0)
    spread = jnp.broadcast_to(spread[None], (XY, 4, 128))

    for copy in copies:
        copy.wait()
    back = gst[...].reshape(CELLS, D)
    pull = lax.dot_general(
        back, w_out[...], (((1,), (1,)), ((), ())), preferred_element_type=F32
    )
    gpre[...] = (pull * slope[...]).astype(BF16)
    for k, target in enumerate((send, keep)):
        left = pl.multiple_of(jnp.where(place[1] == k, HALF, 0), HALF)
        d_out = jnp.dot(
            shidden[...], gst[:, :, pl.ds(left, HALF)].reshape(CELLS, HALF), preferred_element_type=F32
        )
        pulled = gpre[:, pl.ds(left, HALF)]
        d_in = jnp.dot(turned[:D], pulled, preferred_element_type=F32)
        d_noise = jnp.dot(turned[D:], pulled, preferred_element_type=F32)
        for high in range(2):
            pieces = []
            for source, count in ((d_in, 8), (d_out, 8), (d_noise, 2)):
                start = high * XY * count
                for lane in (0, 128):
                    pieces.append(
                        source[start : start + XY * count, lane : lane + 128].reshape(
                            XY, count, 128
                        )
                    )
            pieces.append(spread)
            target[:, high] = jnp.concatenate(pieces, axis=1).astype(BF16)


def three(value):
    high = value.astype(BF16).astype(F32)
    middle = (value - high).astype(BF16).astype(F32)
    return high, middle, (value - high - middle).astype(BF16).astype(F32)


def fold_kernel(arrived, out):
    lanes = lax.broadcasted_iota(jnp.int32, (4, 128), 1)
    first = lax.broadcasted_iota(jnp.int32, (4, 128), 0) == 0
    for high in range(2):
        total = jnp.zeros((SHARE, 128), F32)
        for k in range(XY):
            total = total + arrived[k, high].astype(F32)
        tail = total[LOSS_ROW:]
        row = jnp.sum(tail, axis=0, keepdims=True)
        loss = row[:, :REGIONS] + row[:, REGIONS : 2 * REGIONS] + row[:, 2 * REGIONS : 3 * REGIONS]
        again = jnp.concatenate(
            [*three(loss), jnp.zeros((1, 128 - 3 * REGIONS), F32)], axis=1
        )
        share = jnp.concatenate(
            [total[:LOSS_ROW], jnp.where(first, again, jnp.zeros_like(tail))], axis=0
        ).astype(BF16)
        for k in range(MEMBERS):
            out[high * MEMBERS + k] = share


def last_kernel(arrived, region_loss, grad_in, grad_noise, grad_out):
    for half in range(2):
        total = arrived[half].astype(F32)
        for k in range(1, MEMBERS):
            total = total + arrived[2 * k + half].astype(F32)
        for part in range(2):
            left = half * HALF + part * 128
            grad_in[:, left : left + 128] = total[8 * part : 8 * part + 8]
            grad_out[:, left : left + 128] = total[16 + 8 * part : 24 + 8 * part]
            grad_noise[:, left : left + 128] = total[32 + 2 * part : 34 + 2 * part]
        if half == 0:
            row = total[LOSS_ROW : LOSS_ROW + 1]
            loss = (
                row[:, :REGIONS]
                + row[:, REGIONS : 2 * REGIONS]
                + row[:, 2 * REGIONS : 3 * REGIONS]
            )
            region_loss[...] = loss * (1.0 / (CELLS_ALL // REGIONS * D))


def halos(state, links):
    up = lax.ppermute(state[CELLS - HALO :], TILE, [(i, i + 1) for i in links])
    down = lax.ppermute(state[:HALO], TILE, [(i + 1, i) for i in links])
    return up, down


HBM = pl.BlockSpec(memory_space=pltpu.HBM)
VMEM = pl.BlockSpec(memory_space=pltpu.VMEM)
PARAMS = pltpu.CompilerParams(vmem_limit_bytes=16 * 1024 * 1024)


def in_hbm(array):
    return pltpu.with_memory_space_constraint(array, pltpu.HBM)


def step(
    inputs,
    noise,
    neighbours,
    region_map,
    msg_weight,
    up_weight,
    down_weight,
    student_in,
    student_noise,
    student_out,
):
    state = inputs[0]
    both = pl.pallas_call(
        join_kernel,
        out_shape=jax.ShapeDtypeStruct((CELLS, D + NOISE), BF16),
        in_specs=[HBM] * 2,
        out_specs=HBM,
        scratch_shapes=[
            pltpu.VMEM((CELLS, D + NOISE), BF16),
            pltpu.SemaphoreType.DMA((2 * JOINS,)),
            pltpu.SemaphoreType.DMA((JOINS,)),
        ],
        compiler_params=PARAMS,
        name="join",
    )(in_hbm(state), in_hbm(noise[0]))
    mine = lax.all_to_all(
        both.reshape(MEMBERS, BLOCK, D + NOISE),
        MEMBER,
        split_axis=0,
        concat_axis=0,
        tiled=True,
    )
    top_far, bottom_far = halos(state, [XY - 1])
    top, bottom = halos(state, [i for i in range(TILES - 1) if i != XY - 1])
    middle = pl.pallas_call(
        middle_kernel,
        out_shape=jax.ShapeDtypeStruct((CELLS, D), BF16),
        in_specs=[VMEM] * 2 + [HBM] + [VMEM] * 2,
        out_specs=HBM,
        scratch_shapes=[
            pltpu.VMEM((D, D), BF16),
            pltpu.VMEM((CELLS - 2 * HALO, D), BF16),
            pltpu.SemaphoreType.DMA,
            pltpu.SemaphoreType.DMA((2,)),
        ],
        compiler_params=PARAMS,
        name="middle",
    )
    edges = pl.pallas_call(
        edges_kernel,
        out_shape=jax.ShapeDtypeStruct((CELLS, D), BF16),
        in_specs=[VMEM] * 9 + [HBM],
        out_specs=HBM,
        input_output_aliases={9: 0},
        scratch_shapes=[pltpu.VMEM((2 * HALO, D), BF16), pltpu.SemaphoreType.DMA((2,))],
        compiler_params=PARAMS,
        name="edges",
    )
    partly = middle(state, neighbours, in_hbm(msg_weight), up_weight, down_weight)
    teacher = edges(
        top,
        top_far,
        state,
        bottom,
        bottom_far,
        neighbours,
        msg_weight,
        up_weight,
        down_weight,
        partly,
    )
    every = lax.all_to_all(
        teacher.reshape(MEMBERS, BLOCK, D), MEMBER, split_axis=0, concat_axis=0, tiled=True
    )
    mine = mine.reshape(CELLS, D + NOISE)
    pupil = pl.pallas_call(
        student_kernel,
        out_shape=(
            jax.ShapeDtypeStruct((CELLS, D), BF16),
            jax.ShapeDtypeStruct((H, CELLS), BF16),
            jax.ShapeDtypeStruct((CELLS, H), F32),
            jax.ShapeDtypeStruct((D + NOISE, CELLS), BF16),
        ),
        in_specs=[VMEM] * 4,
        out_specs=[VMEM] * 4,
        compiler_params=PARAMS,
        name="student",
    )
    student, shidden, slope, turned = pupil(mine, student_in, student_noise, student_out)
    place = jnp.stack([region_map[0], lax.axis_index("core").astype(jnp.int32)])
    send, keep = pl.pallas_call(
        score_kernel,
        out_shape=[jax.ShapeDtypeStruct((XY, 2, SHARE, 128), BF16)] * 2,
        in_specs=[VMEM] * 2 + [HBM] * 4 + [pl.BlockSpec(memory_space=pltpu.SMEM)],
        out_specs=[VMEM] * 2,
        scratch_shapes=[
            pltpu.VMEM((MEMBERS, BLOCK, D), BF16),
            pltpu.VMEM((CELLS, D), BF16),
            pltpu.VMEM((16, 128), F32),
            pltpu.VMEM((D + NOISE, CELLS), BF16),
            pltpu.VMEM((H, CELLS), BF16),
            pltpu.VMEM((CELLS, H), F32),
            pltpu.VMEM((H, D), BF16),
            pltpu.SemaphoreType.DMA((4,)),
        ],
        compiler_params=PARAMS,
        name="score",
    )(
        student.reshape(MEMBERS, BLOCK, D),
        every,
        in_hbm(turned),
        in_hbm(shidden),
        in_hbm(slope),
        in_hbm(student_out),
        place,
    )
    other = lax.ppermute(send, "core", [(0, 1), (1, 0)])
    half = (keep.astype(F32) + other.astype(F32)).astype(BF16)
    shares = lax.all_to_all(half, ("tile_1", "tile_2"), split_axis=0, concat_axis=0, tiled=True)
    copies = pl.pallas_call(
        fold_kernel,
        out_shape=jax.ShapeDtypeStruct((2 * MEMBERS, SHARE, 128), BF16),
        in_specs=[VMEM],
        out_specs=VMEM,
        compiler_params=PARAMS,
        name="fold",
    )(shares)
    parts = lax.all_to_all(
        copies, ("tile_0", "member_0", "core"), split_axis=0, concat_axis=0, tiled=True
    )
    region_loss, grad_in, grad_noise, grad_out = pl.pallas_call(
        last_kernel,
        out_shape=[
            jax.ShapeDtypeStruct((1, REGIONS), F32),
            jax.ShapeDtypeStruct((8, D), F32),
            jax.ShapeDtypeStruct((2, D), F32),
            jax.ShapeDtypeStruct((8, D), F32),
        ],
        in_specs=[VMEM],
        out_specs=[VMEM] * 4,
        compiler_params=PARAMS,
        name="last",
    )(parts)
    return (teacher[None], region_loss.reshape(REGIONS), grad_in, grad_noise, grad_out)


def solution(mesh):
    split = Mesh(
        mesh.devices.reshape(4, 2, 2, 4, 8), ("member_0", "core", "tile_0", "tile_1", "tile_2")
    )
    in_specs = (
        P(MEMBER, TILE, None),
        P(MEMBER, TILE, None),
        P(None, TILE),
        P(TILE),
        P(),
        P(),
        P(),
        P(),
        P(),
        P(),
    )
    out_specs = (P(MEMBER, TILE, None), P(), P(TILE, None), P(TILE, None), P(TILE, None))
    return jax.shard_map(step, mesh=split, in_specs=in_specs, out_specs=out_specs, check_vma=False)
```

```python
import math

import jax
import jax.numpy as jnp
from jax import lax
from jax.experimental import pallas as pl
from jax.experimental.pallas import tpu as pltpu
from jax.sharding import Mesh
from jax.sharding import PartitionSpec as P

D = 512
H = 512
NOISE = 128
NBRS = 8
HALO = 64
REGIONS = 8
MEMBERS = 8
CELLS = 512
BLOCK = CELLS // MEMBERS
CELLS_ALL = 32768
TILES = 64
HALF = D // 2
XY = TILES // 2
JOINS = 4
SHARE = 40
LOSS_ROW = 36

MEMBER = ("member_0", "core")
TILE = ("tile_0", "tile_1", "tile_2")
BF16 = jnp.bfloat16
F32 = jnp.float32


def counts(picks, start, rows, width):
    lanes = lax.broadcasted_iota(jnp.int32, (rows, width), 1) + start
    count = jnp.zeros((rows, width), F32)
    for k in range(NBRS):
        count = count + jnp.where(picks[:, k : k + 1] == lanes, 1.0 / NBRS, 0.0)
    return count.astype(BF16)


def teach(state, gathered, msg, up, down):
    resid = state.astype(F32) + jnp.dot(gathered, msg, preferred_element_type=F32)
    power = jnp.mean(resid * resid, axis=1, keepdims=True)
    normed = (resid * lax.rsqrt(power + 1e-06)).astype(BF16)
    hidden = jax.nn.silu(jnp.dot(normed, up, preferred_element_type=F32)).astype(BF16)
    return (resid + jnp.dot(hidden, down, preferred_element_type=F32)).astype(BF16)


def middle_kernel(state, near, msg_at, up, down, out, msg, held, sem, out_sem):
    copy = pltpu.make_async_copy(msg_at, msg, sem)
    copy.start()
    sub = 128
    parts = []
    for at in range(0, CELLS - 2 * HALO, sub):
        picks = near[:, HALO + at : HALO + at + sub].T
        parts.append(
            jnp.dot(
                counts(picks, HALO + at, sub, 2 * sub),
                state[at : at + 2 * sub],
                preferred_element_type=F32,
            ).astype(BF16)
        )
    copy.wait()
    half = (CELLS - 2 * HALO) // 2
    gathered = jnp.concatenate(parts, axis=0)
    writes = []
    for k, at in enumerate((0, half)):
        held[at : at + half] = teach(
            state[HALO + at : HALO + at + half],
            gathered[at : at + half],
            msg[...],
            up[...],
            down[...],
        )
        writes.append(
            pltpu.make_async_copy(
                held.at[at : at + half], out.at[HALO + at : HALO + at + half], out_sem.at[k]
            )
        )
        writes[-1].start()
    for copy in writes:
        copy.wait()


def edges_kernel(odd_swap, even_swap, state, near, msg, up, down, partly, odd, out, held, sem):
    reach = 3 * HALO
    is_odd = jnp.full((HALO, D), odd[0], jnp.int32) == 1
    after_odd = odd_swap[...].astype(F32)
    after_even = even_swap[...].astype(F32)
    top = jnp.where(is_odd, after_even, after_odd).astype(BF16)
    bottom = jnp.where(is_odd, after_odd, after_even).astype(BF16)
    above = jnp.concatenate([top, state[: 2 * HALO]], axis=0)
    below = jnp.concatenate([state[CELLS - 2 * HALO :], bottom], axis=0)
    first = near[:, : 2 * HALO].T[:HALO]
    last = near[:, CELLS - 2 * HALO :].T[HALO:]
    gathered = jnp.concatenate(
        [
            jnp.dot(counts(first, 0, HALO, reach), above, preferred_element_type=F32),
            jnp.dot(
                counts(last, CELLS - HALO, HALO, reach), below, preferred_element_type=F32
            ),
        ],
        axis=0,
    ).astype(BF16)
    ends = jnp.concatenate([state[:HALO], state[CELLS - HALO :]], axis=0)
    held[...] = teach(ends, gathered, msg[...], up[...], down[...])
    writes = [
        pltpu.make_async_copy(held.at[:HALO], out.at[:HALO], sem.at[0]),
        pltpu.make_async_copy(held.at[HALO:], out.at[CELLS - HALO :], sem.at[1]),
    ]
    for copy in writes:
        copy.start()
    for copy in writes:
        copy.wait()


def join_kernel(state, noise, both, held, sem, out_sem):
    rows = CELLS // JOINS
    reads = []
    for k in range(JOINS):
        at = pl.ds(k * rows, rows)
        reads.append(
            (
                pltpu.make_async_copy(state.at[at], held.at[at, :D], sem.at[2 * k]),
                pltpu.make_async_copy(noise.at[at], held.at[at, D:], sem.at[2 * k + 1]),
            )
        )
        for copy in reads[-1]:
            copy.start()
    writes = []
    for k in range(JOINS):
        at = pl.ds(k * rows, rows)
        for copy in reads[k]:
            copy.wait()
        writes.append(pltpu.make_async_copy(held.at[at], both.at[at], out_sem.at[k]))
        writes[-1].start()
    for copy in writes:
        copy.wait()


def student_kernel(mine, w_in, w_noise, w_out, student, shidden, slope, turned):
    rows = 256
    for at in range(0, CELLS, rows):
        state = mine[at : at + rows, :D]
        preact = jnp.dot(state, w_in[...], preferred_element_type=F32) + jnp.dot(
            mine[at : at + rows, D:], w_noise[...], preferred_element_type=F32
        )
        sig = jax.nn.sigmoid(preact)
        hid = (preact * sig).astype(BF16)
        slope[at : at + rows] = sig * (1.0 + preact * (1.0 - sig))
        student[at : at + rows] = (
            state.astype(F32) + jnp.dot(hid, w_out[...], preferred_element_type=F32)
        ).astype(BF16)
        shidden[:, at : at + rows] = hid.T
        turned[:, at : at + rows] = mine[at : at + rows].T


def score_kernel(
    student,
    teacher,
    turned_at,
    shidden_at,
    slope_at,
    w_out_at,
    place,
    send,
    keep,
    gst,
    gpre,
    wide,
    turned,
    shidden,
    slope,
    w_out,
    sem,
):
    copies = [
        pltpu.make_async_copy(source, target, sem.at[k])
        for k, (source, target) in enumerate(
            ((turned_at, turned), (shidden_at, shidden), (slope_at, slope), (w_out_at, w_out))
        )
    ]
    for copy in copies:
        copy.start()
    step = 16
    wide[...] = jnp.zeros_like(wide)

    def block(cell, lane):
        s = [student[m, pl.ds(cell, step), lane : lane + 128].astype(F32) for m in range(MEMBERS)]
        g = [jnp.zeros((step, 128), F32) for _ in range(MEMBERS)]
        loss = jnp.zeros((step, 128), F32)
        for n in range(MEMBERS):
            t = teacher[n, pl.ds(cell, step), lane : lane + 128].astype(F32)
            for m in range(MEMBERS):
                d = s[m] - t
                q = d * d + 0.01
                inv = lax.rsqrt(q)
                loss = loss + q * inv
                g[m] = g[m] + d * inv
        ratio = (MEMBERS - 1) / MEMBERS
        loss = loss * ratio
        g = [x * ratio for x in g]
        for m in range(MEMBERS):
            for n in range(m + 1, MEMBERS):
                d = s[m] - s[n]
                q = d * d + 0.01
                inv = lax.rsqrt(q)
                r = d * inv
                loss = loss - q * inv
                g[m] = g[m] - r
                g[n] = g[n] + r
        scale = 1.0 / (MEMBERS * (MEMBERS - 1) * math.sqrt(CELLS_ALL))
        for m in range(MEMBERS):
            gst[m, pl.ds(cell, step), lane : lane + 128] = (g[m] * scale).astype(BF16)
        pairs = MEMBERS * (MEMBERS - 1)
        wide[...] += (loss - 0.1 * (pairs - pairs // 2)) * (1.0 / pairs)

    def body(i, carry):
        cell = pl.multiple_of(i * step, step)
        for lane in range(0, D, 128):
            block(cell, lane)
        return carry

    lax.fori_loop(0, BLOCK // step, body, 0)

    total = jnp.sum(jnp.sum(wide[...], axis=0, keepdims=True), axis=1, keepdims=True)
    lane_ids = lax.broadcasted_iota(jnp.int32, (4, 128), 1)
    at = jnp.where(lax.broadcasted_iota(jnp.int32, (4, 128), 0) == place[1], place[0], -128)
    spread = jnp.zeros((4, 128), F32)
    for k, piece in enumerate(three(total)):
        spread = spread + jnp.where(lane_ids == at + k * REGIONS, piece, 0.0)
    spread = jnp.broadcast_to(spread[None], (XY, 4, 128))

    for copy in copies:
        copy.wait()
    back = gst[...].reshape(CELLS, D)
    pull = lax.dot_general(
        back, w_out[...], (((1,), (1,)), ((), ())), preferred_element_type=F32
    )
    gpre[...] = (pull * slope[...]).astype(BF16)
    for k, target in enumerate((send, keep)):
        left = pl.multiple_of(jnp.where(place[1] == k, HALF, 0), HALF)
        d_out = jnp.dot(
            shidden[...], gst[:, :, pl.ds(left, HALF)].reshape(CELLS, HALF), preferred_element_type=F32
        )
        pulled = gpre[:, pl.ds(left, HALF)]
        d_in = jnp.dot(turned[:D], pulled, preferred_element_type=F32)
        d_noise = jnp.dot(turned[D:], pulled, preferred_element_type=F32)
        for high in range(2):
            pieces = []
            for source, count in ((d_in, 8), (d_out, 8), (d_noise, 2)):
                start = high * XY * count
                for lane in (0, 128):
                    pieces.append(
                        source[start : start + XY * count, lane : lane + 128].reshape(
                            XY, count, 128
                        )
                    )
            pieces.append(spread)
            target[:, high] = jnp.concatenate(pieces, axis=1).astype(BF16)


def three(value):
    high = value.astype(BF16).astype(F32)
    middle = (value - high).astype(BF16).astype(F32)
    return high, middle, (value - high - middle).astype(BF16).astype(F32)


def fold_kernel(arrived, out):
    lanes = lax.broadcasted_iota(jnp.int32, (4, 128), 1)
    first = lax.broadcasted_iota(jnp.int32, (4, 128), 0) == 0
    for high in range(2):
        total = jnp.zeros((SHARE, 128), F32)
        for k in range(XY):
            total = total + arrived[k, high].astype(F32)
        tail = total[LOSS_ROW:]
        row = jnp.sum(tail, axis=0, keepdims=True)
        loss = row[:, :REGIONS] + row[:, REGIONS : 2 * REGIONS] + row[:, 2 * REGIONS : 3 * REGIONS]
        again = jnp.concatenate(
            [*three(loss), jnp.zeros((1, 128 - 3 * REGIONS), F32)], axis=1
        )
        share = jnp.concatenate(
            [total[:LOSS_ROW], jnp.where(first, again, jnp.zeros_like(tail))], axis=0
        ).astype(BF16)
        for k in range(MEMBERS):
            out[high * MEMBERS + k] = share


def last_kernel(arrived, region_loss, grad_in, grad_noise, grad_out):
    for half in range(2):
        total = arrived[half].astype(F32)
        for k in range(1, MEMBERS):
            total = total + arrived[2 * k + half].astype(F32)
        for part in range(2):
            left = half * HALF + part * 128
            grad_in[:, left : left + 128] = total[8 * part : 8 * part + 8]
            grad_out[:, left : left + 128] = total[16 + 8 * part : 24 + 8 * part]
            grad_noise[:, left : left + 128] = total[32 + 2 * part : 34 + 2 * part]
        if half == 0:
            row = total[LOSS_ROW : LOSS_ROW + 1]
            loss = (
                row[:, :REGIONS]
                + row[:, REGIONS : 2 * REGIONS]
                + row[:, 2 * REGIONS : 3 * REGIONS]
            )
            region_loss[...] = loss * (1.0 / (CELLS_ALL // REGIONS * D))


def exchanged(state, odd, first):
    ahead = odd if first else 1 - odd
    edge = lax.dynamic_slice_in_dim(state, ahead * (CELLS - HALO), HALO, axis=0)
    pairs = [(i, i + 1) for i in range(first, TILES - 1, 2)]
    return lax.ppermute(edge, TILE, pairs + [(b, a) for a, b in pairs])


HBM = pl.BlockSpec(memory_space=pltpu.HBM)
VMEM = pl.BlockSpec(memory_space=pltpu.VMEM)
PARAMS = pltpu.CompilerParams(vmem_limit_bytes=16 * 1024 * 1024)


def in_hbm(array):
    return pltpu.with_memory_space_constraint(array, pltpu.HBM)


def step(
    inputs,
    noise,
    neighbours,
    region_map,
    msg_weight,
    up_weight,
    down_weight,
    student_in,
    student_noise,
    student_out,
):
    state = inputs[0]
    both = pl.pallas_call(
        join_kernel,
        out_shape=jax.ShapeDtypeStruct((CELLS, D + NOISE), BF16),
        in_specs=[HBM] * 2,
        out_specs=HBM,
        scratch_shapes=[
            pltpu.VMEM((CELLS, D + NOISE), BF16),
            pltpu.SemaphoreType.DMA((2 * JOINS,)),
            pltpu.SemaphoreType.DMA((JOINS,)),
        ],
        compiler_params=pltpu.CompilerParams(vmem_limit_bytes=60 * 1024 * 1024),
        name="join",
    )(in_hbm(state), in_hbm(noise[0]))
    mine = lax.all_to_all(
        both.reshape(MEMBERS, BLOCK, D + NOISE),
        MEMBER,
        split_axis=0,
        concat_axis=0,
        tiled=True,
    )
    odd = lax.axis_index("tile_2") % 2
    far = exchanged(state, odd, 1)
    near = exchanged(state, odd, 0)
    middle = pl.pallas_call(
        middle_kernel,
        out_shape=jax.ShapeDtypeStruct((CELLS, D), BF16),
        in_specs=[VMEM] * 2 + [HBM] + [VMEM] * 2,
        out_specs=HBM,
        scratch_shapes=[
            pltpu.VMEM((D, D), BF16),
            pltpu.VMEM((CELLS - 2 * HALO, D), BF16),
            pltpu.SemaphoreType.DMA,
            pltpu.SemaphoreType.DMA((2,)),
        ],
        compiler_params=PARAMS,
        name="middle",
    )
    edges = pl.pallas_call(
        edges_kernel,
        out_shape=jax.ShapeDtypeStruct((CELLS, D), BF16),
        in_specs=[VMEM] * 7 + [HBM, pl.BlockSpec(memory_space=pltpu.SMEM)],
        out_specs=HBM,
        input_output_aliases={7: 0},
        scratch_shapes=[pltpu.VMEM((2 * HALO, D), BF16), pltpu.SemaphoreType.DMA((2,))],
        compiler_params=PARAMS,
        name="edges",
    )
    partly = middle(state, neighbours, in_hbm(msg_weight), up_weight, down_weight)
    teacher = edges(
        far,
        near,
        state,
        neighbours,
        msg_weight,
        up_weight,
        down_weight,
        partly,
        odd.astype(jnp.int32).reshape(1),
    )
    every = lax.all_to_all(
        teacher.reshape(MEMBERS, BLOCK, D), MEMBER, split_axis=0, concat_axis=0, tiled=True
    )
    mine = mine.reshape(CELLS, D + NOISE)
    pupil = pl.pallas_call(
        student_kernel,
        out_shape=(
            jax.ShapeDtypeStruct((CELLS, D), BF16),
            jax.ShapeDtypeStruct((H, CELLS), BF16),
            jax.ShapeDtypeStruct((CELLS, H), F32),
            jax.ShapeDtypeStruct((D + NOISE, CELLS), BF16),
        ),
        in_specs=[VMEM] * 4,
        out_specs=[VMEM] * 4,
        compiler_params=PARAMS,
        name="student",
    )
    student, shidden, slope, turned = pupil(mine, student_in, student_noise, student_out)
    place = jnp.stack([region_map[0], lax.axis_index("core").astype(jnp.int32)])
    send, keep = pl.pallas_call(
        score_kernel,
        out_shape=[jax.ShapeDtypeStruct((XY, 2, SHARE, 128), BF16)] * 2,
        in_specs=[VMEM] * 2 + [HBM] * 4 + [pl.BlockSpec(memory_space=pltpu.SMEM)],
        out_specs=[VMEM] * 2,
        scratch_shapes=[
            pltpu.VMEM((MEMBERS, BLOCK, D), BF16),
            pltpu.VMEM((CELLS, D), BF16),
            pltpu.VMEM((16, 128), F32),
            pltpu.VMEM((D + NOISE, CELLS), BF16),
            pltpu.VMEM((H, CELLS), BF16),
            pltpu.VMEM((CELLS, H), F32),
            pltpu.VMEM((H, D), BF16),
            pltpu.SemaphoreType.DMA((4,)),
        ],
        compiler_params=PARAMS,
        name="score",
    )(
        student.reshape(MEMBERS, BLOCK, D),
        every,
        in_hbm(turned),
        in_hbm(shidden),
        in_hbm(slope),
        in_hbm(student_out),
        place,
    )
    other = lax.ppermute(send, "core", [(0, 1), (1, 0)])
    half = (keep.astype(F32) + other.astype(F32)).astype(BF16)
    shares = lax.all_to_all(half, ("tile_1", "tile_2"), split_axis=0, concat_axis=0, tiled=True)
    copies = pl.pallas_call(
        fold_kernel,
        out_shape=jax.ShapeDtypeStruct((2 * MEMBERS, SHARE, 128), BF16),
        in_specs=[VMEM],
        out_specs=VMEM,
        compiler_params=PARAMS,
        name="fold",
    )(shares)
    parts = lax.all_to_all(
        copies, ("tile_0", "member_0", "core"), split_axis=0, concat_axis=0, tiled=True
    )
    region_loss, grad_in, grad_noise, grad_out = pl.pallas_call(
        last_kernel,
        out_shape=[
            jax.ShapeDtypeStruct((1, REGIONS), F32),
            jax.ShapeDtypeStruct((8, D), F32),
            jax.ShapeDtypeStruct((2, D), F32),
            jax.ShapeDtypeStruct((8, D), F32),
        ],
        in_specs=[VMEM],
        out_specs=[VMEM] * 4,
        compiler_params=PARAMS,
        name="last",
    )(parts)
    return (teacher[None], region_loss.reshape(REGIONS), grad_in, grad_noise, grad_out)


def solution(mesh):
    split = Mesh(
        mesh.devices.reshape(4, 2, 2, 4, 8), ("member_0", "core", "tile_0", "tile_1", "tile_2")
    )
    in_specs = (
        P(MEMBER, TILE, None),
        P(MEMBER, TILE, None),
        P(None, TILE),
        P(TILE),
        P(),
        P(),
        P(),
        P(),
        P(),
        P(),
    )
    out_specs = (P(MEMBER, TILE, None), P(), P(TILE, None), P(TILE, None), P(TILE, None))
    return jax.shard_map(step, mesh=split, in_specs=in_specs, out_specs=out_specs, check_vma=False)
```

```python
import math

import jax
import jax.numpy as jnp
from jax import lax
from jax.experimental import pallas as pl
from jax.experimental.pallas import tpu as pltpu
from jax.sharding import Mesh
from jax.sharding import PartitionSpec as P

D = 512
H = 512
NOISE = 128
NBRS = 8
HALO = 64
REGIONS = 8
MEMBERS = 8
CELLS = 512
BLOCK = CELLS // MEMBERS
CELLS_ALL = 32768
TILES = 64
HALF = D // 2
XY = TILES // 2
JOINS = 4
STEP = 16
SHARE = 40
LOSS_ROW = 36

MEMBER = ("member_0", "core")
TILE = ("tile_0", "tile_1", "tile_2")
BF16 = jnp.bfloat16
F32 = jnp.float32


def counts(picks, start, rows, width):
    lanes = lax.broadcasted_iota(jnp.int32, (rows, width), 1) + start
    count = jnp.zeros((rows, width), F32)
    for k in range(NBRS):
        count = count + jnp.where(picks[:, k : k + 1] == lanes, 1.0 / NBRS, 0.0)
    return count.astype(BF16)


def teach(state, gathered, msg, up, down):
    resid = state.astype(F32) + jnp.dot(gathered, msg, preferred_element_type=F32)
    power = jnp.mean(resid * resid, axis=1, keepdims=True)
    normed = (resid * lax.rsqrt(power + 1e-06)).astype(BF16)
    hidden = jax.nn.silu(jnp.dot(normed, up, preferred_element_type=F32)).astype(BF16)
    return (resid + jnp.dot(hidden, down, preferred_element_type=F32)).astype(BF16)


def middle_kernel(state, near, msg_at, up, down, out, msg, held, sem, out_sem):
    copy = pltpu.make_async_copy(msg_at, msg, sem)
    copy.start()
    sub = 128
    parts = []
    for at in range(0, CELLS - 2 * HALO, sub):
        picks = near[:, HALO + at : HALO + at + sub].T
        parts.append(
            jnp.dot(
                counts(picks, HALO + at, sub, 2 * sub),
                state[at : at + 2 * sub],
                preferred_element_type=F32,
            ).astype(BF16)
        )
    copy.wait()
    half = (CELLS - 2 * HALO) // 2
    gathered = jnp.concatenate(parts, axis=0)
    writes = []
    for k, at in enumerate((0, half)):
        held[at : at + half] = teach(
            state[HALO + at : HALO + at + half],
            gathered[at : at + half],
            msg[...],
            up[...],
            down[...],
        )
        writes.append(
            pltpu.make_async_copy(
                held.at[at : at + half], out.at[HALO + at : HALO + at + half], out_sem.at[k]
            )
        )
        writes[-1].start()
    for copy in writes:
        copy.wait()


def edges_kernel(odd_swap, even_swap, state, near, msg, up, down, partly, odd, out, held, sem):
    reach = 3 * HALO
    is_odd = jnp.full((HALO, D), odd[0], jnp.int32) == 1
    after_odd = odd_swap[...].astype(F32)
    after_even = even_swap[...].astype(F32)
    top = jnp.where(is_odd, after_even, after_odd).astype(BF16)
    bottom = jnp.where(is_odd, after_odd, after_even).astype(BF16)
    above = jnp.concatenate([top, state[: 2 * HALO]], axis=0)
    below = jnp.concatenate([state[CELLS - 2 * HALO :], bottom], axis=0)
    first = near[:, : 2 * HALO].T[:HALO]
    last = near[:, CELLS - 2 * HALO :].T[HALO:]
    gathered = jnp.concatenate(
        [
            jnp.dot(counts(first, 0, HALO, reach), above, preferred_element_type=F32),
            jnp.dot(
                counts(last, CELLS - HALO, HALO, reach), below, preferred_element_type=F32
            ),
        ],
        axis=0,
    ).astype(BF16)
    ends = jnp.concatenate([state[:HALO], state[CELLS - HALO :]], axis=0)
    held[...] = teach(ends, gathered, msg[...], up[...], down[...])
    writes = [
        pltpu.make_async_copy(held.at[:HALO], out.at[:HALO], sem.at[0]),
        pltpu.make_async_copy(held.at[HALO:], out.at[CELLS - HALO :], sem.at[1]),
    ]
    for copy in writes:
        copy.start()
    for copy in writes:
        copy.wait()


def join_kernel(state, noise, both, held, sem, out_sem):
    rows = CELLS // JOINS
    reads = []
    for k in range(JOINS):
        at = pl.ds(k * rows, rows)
        reads.append(
            (
                pltpu.make_async_copy(state.at[at], held.at[at, :D], sem.at[2 * k]),
                pltpu.make_async_copy(noise.at[at], held.at[at, D:], sem.at[2 * k + 1]),
            )
        )
        for copy in reads[-1]:
            copy.start()
    writes = []
    for k in range(JOINS):
        at = pl.ds(k * rows, rows)
        for copy in reads[k]:
            copy.wait()
        writes.append(pltpu.make_async_copy(held.at[at], both.at[at], out_sem.at[k]))
        writes[-1].start()
    for copy in writes:
        copy.wait()


def student_kernel(
    mine, w_in, w_noise, w_out, shidden, slope, turned, held, within_loss
):
    rows = 256
    for at in range(0, CELLS, rows):
        state = mine[at : at + rows, :D]
        preact = jnp.dot(state, w_in[...], preferred_element_type=F32) + jnp.dot(
            mine[at : at + rows, D:], w_noise[...], preferred_element_type=F32
        )
        sig = jax.nn.sigmoid(preact)
        hid = (preact * sig).astype(BF16)
        slope[at : at + rows] = sig * (1.0 + preact * (1.0 - sig))
        made = (
            state.astype(F32) + jnp.dot(hid, w_out[...], preferred_element_type=F32)
        ).astype(BF16).astype(F32)
        for k in range(rows // BLOCK):
            held[0, at // BLOCK + k] = made[k * BLOCK : (k + 1) * BLOCK]
        shidden[:, at : at + rows] = hid.T
        turned[:, at : at + rows] = mine[at : at + rows].T

    within_loss[...] = jnp.zeros_like(within_loss)

    def body(i, carry):
        cell = pl.multiple_of(i * STEP, STEP)
        for lane in range(0, D, 128):
            at = (pl.ds(cell, STEP), slice(lane, lane + 128))
            s = [held[0, m, at[0], at[1]] for m in range(MEMBERS)]
            g = [jnp.zeros((STEP, 128), F32) for _ in range(MEMBERS)]
            loss = jnp.zeros((STEP, 128), F32)
            for m in range(MEMBERS):
                for n in range(m + 1, MEMBERS):
                    d = s[m] - s[n]
                    q = d * d + 0.01
                    inv = lax.rsqrt(q)
                    r = d * inv
                    loss = loss + q * inv
                    g[m] = g[m] - r
                    g[n] = g[n] + r
            for m in range(MEMBERS):
                held[1, m, at[0], at[1]] = g[m]
            within_loss[...] += loss
        return carry

    lax.fori_loop(0, BLOCK // STEP, body, 0)


def score_kernel(
    held,
    teacher,
    within_loss,
    turned_at,
    shidden_at,
    slope_at,
    w_out_at,
    place,
    send,
    keep,
    gst,
    gpre,
    wide,
    turned,
    shidden,
    slope,
    w_out,
    sem,
):
    copies = [
        pltpu.make_async_copy(source, target, sem.at[k])
        for k, (source, target) in enumerate(
            ((turned_at, turned), (shidden_at, shidden), (slope_at, slope), (w_out_at, w_out))
        )
    ]
    for copy in copies:
        copy.start()
    ratio = (MEMBERS - 1) / MEMBERS
    pairs = MEMBERS * (MEMBERS - 1)
    scale = 1.0 / (pairs * math.sqrt(CELLS_ALL))
    wide[...] = -within_loss[...] * (1.0 / pairs)

    def block(cell, lane):
        s = [held[0, m, pl.ds(cell, STEP), lane : lane + 128] for m in range(MEMBERS)]
        g = [jnp.zeros((STEP, 128), F32) for _ in range(MEMBERS)]
        loss = jnp.zeros((STEP, 128), F32)
        for n in range(MEMBERS):
            t = teacher[n, pl.ds(cell, STEP), lane : lane + 128].astype(F32)
            for m in range(MEMBERS):
                d = s[m] - t
                q = d * d + 0.01
                inv = lax.rsqrt(q)
                loss = loss + q * inv
                g[m] = g[m] + d * inv
        for m in range(MEMBERS):
            total = g[m] * ratio + held[1, m, pl.ds(cell, STEP), lane : lane + 128]
            gst[m, pl.ds(cell, STEP), lane : lane + 128] = (total * scale).astype(BF16)
        wide[...] += (loss * ratio - 0.1 * (pairs - pairs // 2)) * (1.0 / pairs)

    def body(i, carry):
        cell = pl.multiple_of(i * STEP, STEP)
        for lane in range(0, D, 128):
            block(cell, lane)
        return carry

    lax.fori_loop(0, BLOCK // STEP, body, 0)

    total = jnp.sum(jnp.sum(wide[...], axis=0, keepdims=True), axis=1, keepdims=True)
    lane_ids = lax.broadcasted_iota(jnp.int32, (4, 128), 1)
    at = jnp.where(lax.broadcasted_iota(jnp.int32, (4, 128), 0) == place[1], place[0], -128)
    spread = jnp.zeros((4, 128), F32)
    for k, piece in enumerate(three(total)):
        spread = spread + jnp.where(lane_ids == at + k * REGIONS, piece, 0.0)
    spread = jnp.broadcast_to(spread[None], (XY, 4, 128))

    for copy in copies:
        copy.wait()
    back = gst[...].reshape(CELLS, D)
    pull = lax.dot_general(
        back, w_out[...], (((1,), (1,)), ((), ())), preferred_element_type=F32
    )
    gpre[...] = (pull * slope[...]).astype(BF16)
    for k, target in enumerate((send, keep)):
        left = pl.multiple_of(jnp.where(place[1] == k, HALF, 0), HALF)
        d_out = jnp.dot(
            shidden[...], gst[:, :, pl.ds(left, HALF)].reshape(CELLS, HALF), preferred_element_type=F32
        )
        pulled = gpre[:, pl.ds(left, HALF)]
        d_in = jnp.dot(turned[:D], pulled, preferred_element_type=F32)
        d_noise = jnp.dot(turned[D:], pulled, preferred_element_type=F32)
        for high in range(2):
            pieces = []
            for source, count in ((d_in, 8), (d_out, 8), (d_noise, 2)):
                start = high * XY * count
                for lane in (0, 128):
                    pieces.append(
                        source[start : start + XY * count, lane : lane + 128].reshape(
                            XY, count, 128
                        )
                    )
            pieces.append(spread)
            target[:, high] = jnp.concatenate(pieces, axis=1).astype(BF16)


def three(value):
    high = value.astype(BF16).astype(F32)
    middle = (value - high).astype(BF16).astype(F32)
    return high, middle, (value - high - middle).astype(BF16).astype(F32)


def fold_kernel(arrived, out):
    lanes = lax.broadcasted_iota(jnp.int32, (4, 128), 1)
    first = lax.broadcasted_iota(jnp.int32, (4, 128), 0) == 0
    for high in range(2):
        total = jnp.zeros((SHARE, 128), F32)
        for k in range(XY):
            total = total + arrived[k, high].astype(F32)
        tail = total[LOSS_ROW:]
        row = jnp.sum(tail, axis=0, keepdims=True)
        loss = row[:, :REGIONS] + row[:, REGIONS : 2 * REGIONS] + row[:, 2 * REGIONS : 3 * REGIONS]
        again = jnp.concatenate(
            [*three(loss), jnp.zeros((1, 128 - 3 * REGIONS), F32)], axis=1
        )
        share = jnp.concatenate(
            [total[:LOSS_ROW], jnp.where(first, again, jnp.zeros_like(tail))], axis=0
        ).astype(BF16)
        for k in range(MEMBERS):
            out[high * MEMBERS + k] = share


def last_kernel(arrived, region_loss, grad_in, grad_noise, grad_out):
    for half in range(2):
        total = arrived[half].astype(F32)
        for k in range(1, MEMBERS):
            total = total + arrived[2 * k + half].astype(F32)
        for part in range(2):
            left = half * HALF + part * 128
            grad_in[:, left : left + 128] = total[8 * part : 8 * part + 8]
            grad_out[:, left : left + 128] = total[16 + 8 * part : 24 + 8 * part]
            grad_noise[:, left : left + 128] = total[32 + 2 * part : 34 + 2 * part]
        if half == 0:
            row = total[LOSS_ROW : LOSS_ROW + 1]
            loss = (
                row[:, :REGIONS]
                + row[:, REGIONS : 2 * REGIONS]
                + row[:, 2 * REGIONS : 3 * REGIONS]
            )
            region_loss[...] = loss * (1.0 / (CELLS_ALL // REGIONS * D))


def exchanged(state, odd, first):
    ahead = odd if first else 1 - odd
    edge = lax.dynamic_slice_in_dim(state, ahead * (CELLS - HALO), HALO, axis=0)
    pairs = [(i, i + 1) for i in range(first, TILES - 1, 2)]
    return lax.ppermute(edge, TILE, pairs + [(b, a) for a, b in pairs])


HBM = pl.BlockSpec(memory_space=pltpu.HBM)
VMEM = pl.BlockSpec(memory_space=pltpu.VMEM)
PARAMS = pltpu.CompilerParams(vmem_limit_bytes=16 * 1024 * 1024)


def in_hbm(array):
    return pltpu.with_memory_space_constraint(array, pltpu.HBM)


def step(
    inputs,
    noise,
    neighbours,
    region_map,
    msg_weight,
    up_weight,
    down_weight,
    student_in,
    student_noise,
    student_out,
):
    state = inputs[0]
    both = pl.pallas_call(
        join_kernel,
        out_shape=jax.ShapeDtypeStruct((CELLS, D + NOISE), BF16),
        in_specs=[HBM] * 2,
        out_specs=HBM,
        scratch_shapes=[
            pltpu.VMEM((CELLS, D + NOISE), BF16),
            pltpu.SemaphoreType.DMA((2 * JOINS,)),
            pltpu.SemaphoreType.DMA((JOINS,)),
        ],
        compiler_params=pltpu.CompilerParams(vmem_limit_bytes=60 * 1024 * 1024),
        name="join",
    )(in_hbm(state), in_hbm(noise[0]))
    mine = lax.all_to_all(
        both.reshape(MEMBERS, BLOCK, D + NOISE),
        MEMBER,
        split_axis=0,
        concat_axis=0,
        tiled=True,
    )
    odd = lax.axis_index("tile_2") % 2
    far = exchanged(state, odd, 1)
    near = exchanged(state, odd, 0)
    middle = pl.pallas_call(
        middle_kernel,
        out_shape=jax.ShapeDtypeStruct((CELLS, D), BF16),
        in_specs=[VMEM] * 2 + [HBM] + [VMEM] * 2,
        out_specs=HBM,
        scratch_shapes=[
            pltpu.VMEM((D, D), BF16),
            pltpu.VMEM((CELLS - 2 * HALO, D), BF16),
            pltpu.SemaphoreType.DMA,
            pltpu.SemaphoreType.DMA((2,)),
        ],
        compiler_params=PARAMS,
        name="middle",
    )
    edges = pl.pallas_call(
        edges_kernel,
        out_shape=jax.ShapeDtypeStruct((CELLS, D), BF16),
        in_specs=[VMEM] * 7 + [HBM, pl.BlockSpec(memory_space=pltpu.SMEM)],
        out_specs=HBM,
        input_output_aliases={7: 0},
        scratch_shapes=[pltpu.VMEM((2 * HALO, D), BF16), pltpu.SemaphoreType.DMA((2,))],
        compiler_params=PARAMS,
        name="edges",
    )
    partly = middle(state, neighbours, in_hbm(msg_weight), up_weight, down_weight)
    teacher = edges(
        far,
        near,
        state,
        neighbours,
        msg_weight,
        up_weight,
        down_weight,
        partly,
        odd.astype(jnp.int32).reshape(1),
    )
    every = lax.all_to_all(
        teacher.reshape(MEMBERS, BLOCK, D), MEMBER, split_axis=0, concat_axis=0, tiled=True
    )
    mine = mine.reshape(CELLS, D + NOISE)
    pupil = pl.pallas_call(
        student_kernel,
        out_shape=(
            jax.ShapeDtypeStruct((H, CELLS), BF16),
            jax.ShapeDtypeStruct((CELLS, H), F32),
            jax.ShapeDtypeStruct((D + NOISE, CELLS), BF16),
            jax.ShapeDtypeStruct((2, MEMBERS, BLOCK, D), F32),
            jax.ShapeDtypeStruct((STEP, 128), F32),
        ),
        in_specs=[VMEM] * 4,
        out_specs=[VMEM] * 5,
        compiler_params=PARAMS,
        name="student",
    )
    shidden, slope, turned, held, within_loss = pupil(mine, student_in, student_noise, student_out)
    place = jnp.stack([region_map[0], lax.axis_index("core").astype(jnp.int32)])
    send, keep = pl.pallas_call(
        score_kernel,
        out_shape=[jax.ShapeDtypeStruct((XY, 2, SHARE, 128), BF16)] * 2,
        in_specs=[VMEM] * 3 + [HBM] * 4 + [pl.BlockSpec(memory_space=pltpu.SMEM)],
        out_specs=[VMEM] * 2,
        scratch_shapes=[
            pltpu.VMEM((MEMBERS, BLOCK, D), BF16),
            pltpu.VMEM((CELLS, D), BF16),
            pltpu.VMEM((STEP, 128), F32),
            pltpu.VMEM((D + NOISE, CELLS), BF16),
            pltpu.VMEM((H, CELLS), BF16),
            pltpu.VMEM((CELLS, H), F32),
            pltpu.VMEM((H, D), BF16),
            pltpu.SemaphoreType.DMA((4,)),
        ],
        compiler_params=PARAMS,
        name="score",
    )(
        held,
        every,
        within_loss,
        in_hbm(turned),
        in_hbm(shidden),
        in_hbm(slope),
        in_hbm(student_out),
        place,
    )
    other = lax.ppermute(send, "core", [(0, 1), (1, 0)])
    half = (keep.astype(F32) + other.astype(F32)).astype(BF16)
    shares = lax.all_to_all(half, ("tile_1", "tile_2"), split_axis=0, concat_axis=0, tiled=True)
    copies = pl.pallas_call(
        fold_kernel,
        out_shape=jax.ShapeDtypeStruct((2 * MEMBERS, SHARE, 128), BF16),
        in_specs=[VMEM],
        out_specs=VMEM,
        compiler_params=PARAMS,
        name="fold",
    )(shares)
    parts = lax.all_to_all(
        copies, ("tile_0", "member_0", "core"), split_axis=0, concat_axis=0, tiled=True
    )
    region_loss, grad_in, grad_noise, grad_out = pl.pallas_call(
        last_kernel,
        out_shape=[
            jax.ShapeDtypeStruct((1, REGIONS), F32),
            jax.ShapeDtypeStruct((8, D), F32),
            jax.ShapeDtypeStruct((2, D), F32),
            jax.ShapeDtypeStruct((8, D), F32),
        ],
        in_specs=[VMEM],
        out_specs=[VMEM] * 4,
        compiler_params=PARAMS,
        name="last",
    )(parts)
    return (teacher[None], region_loss.reshape(REGIONS), grad_in, grad_noise, grad_out)


def solution(mesh):
    split = Mesh(
        mesh.devices.reshape(4, 2, 2, 4, 8), ("member_0", "core", "tile_0", "tile_1", "tile_2")
    )
    in_specs = (
        P(MEMBER, TILE, None),
        P(MEMBER, TILE, None),
        P(None, TILE),
        P(TILE),
        P(),
        P(),
        P(),
        P(),
        P(),
        P(),
    )
    out_specs = (P(MEMBER, TILE, None), P(), P(TILE, None), P(TILE, None), P(TILE, None))
    return jax.shard_map(step, mesh=split, in_specs=in_specs, out_specs=out_specs, check_vma=False)
```

```python
import math

import jax
import jax.numpy as jnp
from jax import lax
from jax.experimental import pallas as pl
from jax.experimental.pallas import tpu as pltpu
from jax.sharding import Mesh
from jax.sharding import PartitionSpec as P

D = 512
FF = 1024
H = 512
NOISE = 128
NBRS = 8
HALO = 64
REGIONS = 8
MEMBERS = 8
CELLS = 512
BLOCK = CELLS // MEMBERS
CELLS_ALL = 32768
TILES = 64
HALF = D // 2
XY = TILES // 2
SHARE = 40
LOSS_ROW = 36

MEMBER = ("member_0", "core")
TILE = ("tile_0", "tile_1", "tile_2")
BF16 = jnp.bfloat16
F32 = jnp.float32


def counts(picks, start, rows, width):
    lanes = lax.broadcasted_iota(jnp.int32, (rows, width), 1) + start
    count = jnp.zeros((rows, width), F32)
    for k in range(NBRS):
        count = count + jnp.where(picks[:, k : k + 1] == lanes, 1.0 / NBRS, 0.0)
    return count.astype(BF16)


def teach(state, gathered, msg, up, down):
    resid = state.astype(F32) + jnp.dot(gathered, msg, preferred_element_type=F32)
    power = jnp.mean(resid * resid, axis=1, keepdims=True)
    normed = (resid * lax.rsqrt(power + 1e-06)).astype(BF16)
    hidden = jax.nn.silu(jnp.dot(normed, up, preferred_element_type=F32)).astype(BF16)
    return (resid + jnp.dot(hidden, down, preferred_element_type=F32)).astype(BF16)


def middle_kernel(
    state,
    noise,
    near,
    msg_at,
    up_at,
    down_at,
    out,
    sent,
    msg,
    up,
    down,
    held,
    sem,
    out_sem,
    noise_sem,
):
    loads = [
        pltpu.make_async_copy(source, target, sem.at[k])
        for k, (source, target) in enumerate(((msg_at, msg), (up_at, up), (down_at, down)))
    ]
    for copy in loads:
        copy.start()
    beside = pltpu.make_async_copy(noise, sent.at[:, D:], noise_sem)
    beside.start()
    sub = 128
    parts = []
    for at in range(0, CELLS - 2 * HALO, sub):
        picks = near[:, HALO + at : HALO + at + sub].T
        parts.append(
            jnp.dot(
                counts(picks, HALO + at, sub, 2 * sub),
                state[at : at + 2 * sub],
                preferred_element_type=F32,
            ).astype(BF16)
        )
    for copy in loads:
        copy.wait()
    half = (CELLS - 2 * HALO) // 2
    gathered = jnp.concatenate(parts, axis=0)
    writes = []
    for k, at in enumerate((0, half)):
        held[at : at + half] = teach(
            state[HALO + at : HALO + at + half],
            gathered[at : at + half],
            msg[...],
            up[...],
            down[...],
        )
        rows = pl.ds(HALO + at, half)
        for target, wait in ((out.at[rows], 2 * k), (sent.at[rows, :D], 2 * k + 1)):
            writes.append(
                pltpu.make_async_copy(held.at[at : at + half], target, out_sem.at[wait])
            )
            writes[-1].start()
    beside.wait()
    for copy in writes:
        copy.wait()


def edges_kernel(
    odd_swap,
    even_swap,
    state,
    near,
    msg,
    up,
    down,
    partly,
    partly_sent,
    odd,
    out,
    sent,
    held,
    sem,
):
    reach = 3 * HALO
    is_odd = jnp.full((HALO, D), odd[0], jnp.int32) == 1
    after_odd = odd_swap[...].astype(F32)
    after_even = even_swap[...].astype(F32)
    top = jnp.where(is_odd, after_even, after_odd).astype(BF16)
    bottom = jnp.where(is_odd, after_odd, after_even).astype(BF16)
    above = jnp.concatenate([top, state[: 2 * HALO]], axis=0)
    below = jnp.concatenate([state[CELLS - 2 * HALO :], bottom], axis=0)
    first = near[:, : 2 * HALO].T[:HALO]
    last = near[:, CELLS - 2 * HALO :].T[HALO:]
    gathered = jnp.concatenate(
        [
            jnp.dot(counts(first, 0, HALO, reach), above, preferred_element_type=F32),
            jnp.dot(
                counts(last, CELLS - HALO, HALO, reach), below, preferred_element_type=F32
            ),
        ],
        axis=0,
    ).astype(BF16)
    ends = jnp.concatenate([state[:HALO], state[CELLS - HALO :]], axis=0)
    held[...] = teach(ends, gathered, msg[...], up[...], down[...])
    writes = [
        pltpu.make_async_copy(held.at[:HALO], out.at[:HALO], sem.at[0]),
        pltpu.make_async_copy(held.at[HALO:], out.at[CELLS - HALO :], sem.at[1]),
        pltpu.make_async_copy(held.at[:HALO], sent.at[:HALO, :D], sem.at[2]),
        pltpu.make_async_copy(held.at[HALO:], sent.at[CELLS - HALO :, :D], sem.at[3]),
    ]
    for copy in writes:
        copy.start()
    for copy in writes:
        copy.wait()


def student_kernel(mine, w_in, early, turned):
    rows = 256
    for at in range(0, CELLS, rows):
        state = mine[at : at + rows]
        early[at : at + rows] = jnp.dot(state, w_in[...], preferred_element_type=F32)
        turned[:, at : at + rows] = state.T


def score_kernel(
    early,
    mine,
    every,
    w_noise,
    w_out,
    turned_at,
    place,
    send,
    keep,
    gst,
    gpre,
    wide,
    turned,
    turned_noise,
    shidden,
    slope,
    student,
    sem,
):
    copy = pltpu.make_async_copy(turned_at, turned, sem)
    copy.start()
    rows = 256
    for at in range(0, CELLS, rows):
        draws = every[at // BLOCK : (at + rows) // BLOCK, :, D:].reshape(rows, NOISE)
        preact = early[at : at + rows] + jnp.dot(
            draws, w_noise[...], preferred_element_type=F32
        )
        sig = jax.nn.sigmoid(preact)
        hid = (preact * sig).astype(BF16)
        slope[at : at + rows] = sig * (1.0 + preact * (1.0 - sig))
        student[at : at + rows] = (
            mine[at : at + rows].astype(F32)
            + jnp.dot(hid, w_out[...], preferred_element_type=F32)
        ).astype(BF16)
        shidden[:, at : at + rows] = hid.T
        turned_noise[:, at : at + rows] = draws.T

    step = 16
    wide[...] = jnp.zeros_like(wide)

    def block(cell, lane):
        s = [
            student[pl.ds(cell + m * BLOCK, step), lane : lane + 128].astype(F32)
            for m in range(MEMBERS)
        ]
        g = [jnp.zeros((step, 128), F32) for _ in range(MEMBERS)]
        loss = jnp.zeros((step, 128), F32)
        for n in range(MEMBERS):
            t = every[n, pl.ds(cell, step), lane : lane + 128].astype(F32)
            for m in range(MEMBERS):
                d = s[m] - t
                q = d * d + 0.01
                inv = lax.rsqrt(q)
                loss = loss + q * inv
                g[m] = g[m] + d * inv
        ratio = (MEMBERS - 1) / MEMBERS
        loss = loss * ratio
        g = [x * ratio for x in g]
        for m in range(MEMBERS):
            for n in range(m + 1, MEMBERS):
                d = s[m] - s[n]
                q = d * d + 0.01
                inv = lax.rsqrt(q)
                r = d * inv
                loss = loss - q * inv
                g[m] = g[m] - r
                g[n] = g[n] + r
        scale = 1.0 / (MEMBERS * (MEMBERS - 1) * math.sqrt(CELLS_ALL))
        for m in range(MEMBERS):
            gst[m, pl.ds(cell, step), lane : lane + 128] = (g[m] * scale).astype(BF16)
        pairs = MEMBERS * (MEMBERS - 1)
        wide[...] += (loss - 0.1 * (pairs - pairs // 2)) * (1.0 / pairs)

    def body(i, carry):
        cell = pl.multiple_of(i * step, step)
        for lane in range(0, D, 128):
            block(cell, lane)
        return carry

    lax.fori_loop(0, BLOCK // step, body, 0)

    total = jnp.sum(jnp.sum(wide[...], axis=0, keepdims=True), axis=1, keepdims=True)
    lane_ids = lax.broadcasted_iota(jnp.int32, (4, 128), 1)
    at = jnp.where(lax.broadcasted_iota(jnp.int32, (4, 128), 0) == place[1], place[0], -128)
    spread = jnp.zeros((4, 128), F32)
    for k, piece in enumerate(three(total)):
        spread = spread + jnp.where(lane_ids == at + k * REGIONS, piece, 0.0)
    spread = jnp.broadcast_to(spread[None], (XY, 4, 128))

    copy.wait()
    back = gst[...].reshape(CELLS, D)
    pull = lax.dot_general(
        back, w_out[...], (((1,), (1,)), ((), ())), preferred_element_type=F32
    )
    gpre[...] = (pull * slope[...]).astype(BF16)
    for k, target in enumerate((send, keep)):
        left = pl.multiple_of(jnp.where(place[1] == k, HALF, 0), HALF)
        d_out = jnp.dot(
            shidden[...], gst[:, :, pl.ds(left, HALF)].reshape(CELLS, HALF), preferred_element_type=F32
        )
        pulled = gpre[:, pl.ds(left, HALF)]
        d_in = jnp.dot(turned[...], pulled, preferred_element_type=F32)
        d_noise = jnp.dot(turned_noise[...], pulled, preferred_element_type=F32)
        for high in range(2):
            pieces = []
            for source, count in ((d_in, 8), (d_out, 8), (d_noise, 2)):
                start = high * XY * count
                for lane in (0, 128):
                    pieces.append(
                        source[start : start + XY * count, lane : lane + 128].reshape(
                            XY, count, 128
                        )
                    )
            pieces.append(spread)
            target[:, high] = jnp.concatenate(pieces, axis=1).astype(BF16)


def three(value):
    high = value.astype(BF16).astype(F32)
    middle = (value - high).astype(BF16).astype(F32)
    return high, middle, (value - high - middle).astype(BF16).astype(F32)


def fold_kernel(arrived, out):
    lanes = lax.broadcasted_iota(jnp.int32, (4, 128), 1)
    first = lax.broadcasted_iota(jnp.int32, (4, 128), 0) == 0
    for high in range(2):
        total = jnp.zeros((SHARE, 128), F32)
        for k in range(XY):
            total = total + arrived[k, high].astype(F32)
        tail = total[LOSS_ROW:]
        row = jnp.sum(tail, axis=0, keepdims=True)
        loss = row[:, :REGIONS] + row[:, REGIONS : 2 * REGIONS] + row[:, 2 * REGIONS : 3 * REGIONS]
        again = jnp.concatenate(
            [*three(loss), jnp.zeros((1, 128 - 3 * REGIONS), F32)], axis=1
        )
        share = jnp.concatenate(
            [total[:LOSS_ROW], jnp.where(first, again, jnp.zeros_like(tail))], axis=0
        ).astype(BF16)
        for k in range(MEMBERS):
            out[high * MEMBERS + k] = share


def last_kernel(arrived, region_loss, grad_in, grad_noise, grad_out):
    for half in range(2):
        total = arrived[half].astype(F32)
        for k in range(1, MEMBERS):
            total = total + arrived[2 * k + half].astype(F32)
        for part in range(2):
            left = half * HALF + part * 128
            grad_in[:, left : left + 128] = total[8 * part : 8 * part + 8]
            grad_out[:, left : left + 128] = total[16 + 8 * part : 24 + 8 * part]
            grad_noise[:, left : left + 128] = total[32 + 2 * part : 34 + 2 * part]
        if half == 0:
            row = total[LOSS_ROW : LOSS_ROW + 1]
            loss = (
                row[:, :REGIONS]
                + row[:, REGIONS : 2 * REGIONS]
                + row[:, 2 * REGIONS : 3 * REGIONS]
            )
            region_loss[...] = loss * (1.0 / (CELLS_ALL // REGIONS * D))


def exchanged(state, odd, first):
    ahead = odd if first else 1 - odd
    edge = lax.dynamic_slice_in_dim(state, ahead * (CELLS - HALO), HALO, axis=0)
    pairs = [(i, i + 1) for i in range(first, TILES - 1, 2)]
    return lax.ppermute(edge, TILE, pairs + [(b, a) for a, b in pairs])


HBM = pl.BlockSpec(memory_space=pltpu.HBM)
VMEM = pl.BlockSpec(memory_space=pltpu.VMEM)
PARAMS = pltpu.CompilerParams(vmem_limit_bytes=16 * 1024 * 1024)


def in_hbm(array):
    return pltpu.with_memory_space_constraint(array, pltpu.HBM)


def step(
    inputs,
    noise,
    neighbours,
    region_map,
    msg_weight,
    up_weight,
    down_weight,
    student_in,
    student_noise,
    student_out,
):
    state = inputs[0]
    mine = lax.all_to_all(
        state.reshape(MEMBERS, BLOCK, D), MEMBER, split_axis=0, concat_axis=0, tiled=True
    )
    odd = lax.axis_index("tile_2") % 2
    far = exchanged(state, odd, 1)
    near = exchanged(state, odd, 0)
    shapes = (
        jax.ShapeDtypeStruct((CELLS, D), BF16),
        jax.ShapeDtypeStruct((CELLS, D + NOISE), BF16),
    )
    middle = pl.pallas_call(
        middle_kernel,
        out_shape=shapes,
        in_specs=[VMEM] * 3 + [HBM] * 3,
        out_specs=[HBM] * 2,
        scratch_shapes=[
            pltpu.VMEM((D, D), BF16),
            pltpu.VMEM((D, FF), BF16),
            pltpu.VMEM((FF, D), BF16),
            pltpu.VMEM((CELLS - 2 * HALO, D), BF16),
            pltpu.SemaphoreType.DMA((3,)),
            pltpu.SemaphoreType.DMA((4,)),
            pltpu.SemaphoreType.DMA,
        ],
        compiler_params=PARAMS,
        name="middle",
    )
    edges = pl.pallas_call(
        edges_kernel,
        out_shape=shapes,
        in_specs=[VMEM] * 7 + [HBM] * 2 + [pl.BlockSpec(memory_space=pltpu.SMEM)],
        out_specs=[HBM] * 2,
        input_output_aliases={7: 0, 8: 1},
        scratch_shapes=[pltpu.VMEM((2 * HALO, D), BF16), pltpu.SemaphoreType.DMA((4,))],
        compiler_params=PARAMS,
        name="edges",
    )
    partly, partly_sent = middle(
        state,
        noise[0],
        neighbours,
        in_hbm(msg_weight),
        in_hbm(up_weight),
        in_hbm(down_weight),
    )
    teacher, sent = edges(
        far,
        near,
        state,
        neighbours,
        msg_weight,
        up_weight,
        down_weight,
        partly,
        partly_sent,
        odd.astype(jnp.int32).reshape(1),
    )
    every = lax.all_to_all(
        sent.reshape(MEMBERS, BLOCK, D + NOISE),
        MEMBER,
        split_axis=0,
        concat_axis=0,
        tiled=True,
    )
    mine = mine.reshape(CELLS, D)
    pupil = pl.pallas_call(
        student_kernel,
        out_shape=(
            jax.ShapeDtypeStruct((CELLS, H), F32),
            jax.ShapeDtypeStruct((D, CELLS), BF16),
        ),
        in_specs=[VMEM] * 2,
        out_specs=[VMEM] * 2,
        compiler_params=PARAMS,
        name="student",
    )
    early, turned = pupil(mine, student_in)
    place = jnp.stack([region_map[0], lax.axis_index("core").astype(jnp.int32)])
    send, keep = pl.pallas_call(
        score_kernel,
        out_shape=[jax.ShapeDtypeStruct((XY, 2, SHARE, 128), BF16)] * 2,
        in_specs=[VMEM] * 5 + [HBM, pl.BlockSpec(memory_space=pltpu.SMEM)],
        out_specs=[VMEM] * 2,
        scratch_shapes=[
            pltpu.VMEM((MEMBERS, BLOCK, D), BF16),
            pltpu.VMEM((CELLS, D), BF16),
            pltpu.VMEM((16, 128), F32),
            pltpu.VMEM((D, CELLS), BF16),
            pltpu.VMEM((NOISE, CELLS), BF16),
            pltpu.VMEM((H, CELLS), BF16),
            pltpu.VMEM((CELLS, H), F32),
            pltpu.VMEM((CELLS, D), BF16),
            pltpu.SemaphoreType.DMA,
        ],
        compiler_params=PARAMS,
        name="score",
    )(early, mine, every, student_noise, student_out, in_hbm(turned), place)
    other = lax.ppermute(send, "core", [(0, 1), (1, 0)])
    half = (keep.astype(F32) + other.astype(F32)).astype(BF16)
    shares = lax.all_to_all(half, ("tile_1", "tile_2"), split_axis=0, concat_axis=0, tiled=True)
    copies = pl.pallas_call(
        fold_kernel,
        out_shape=jax.ShapeDtypeStruct((2 * MEMBERS, SHARE, 128), BF16),
        in_specs=[VMEM],
        out_specs=VMEM,
        compiler_params=PARAMS,
        name="fold",
    )(shares)
    parts = lax.all_to_all(
        copies, ("tile_0", "member_0", "core"), split_axis=0, concat_axis=0, tiled=True
    )
    region_loss, grad_in, grad_noise, grad_out = pl.pallas_call(
        last_kernel,
        out_shape=[
            jax.ShapeDtypeStruct((1, REGIONS), F32),
            jax.ShapeDtypeStruct((8, D), F32),
            jax.ShapeDtypeStruct((2, D), F32),
            jax.ShapeDtypeStruct((8, D), F32),
        ],
        in_specs=[VMEM],
        out_specs=[VMEM] * 4,
        compiler_params=PARAMS,
        name="last",
    )(parts)
    return (teacher[None], region_loss.reshape(REGIONS), grad_in, grad_noise, grad_out)


def solution(mesh):
    split = Mesh(
        mesh.devices.reshape(4, 2, 2, 4, 8), ("member_0", "core", "tile_0", "tile_1", "tile_2")
    )
    in_specs = (
        P(MEMBER, TILE, None),
        P(MEMBER, TILE, None),
        P(None, TILE),
        P(TILE),
        P(),
        P(),
        P(),
        P(),
        P(),
        P(),
    )
    out_specs = (P(MEMBER, TILE, None), P(), P(TILE, None), P(TILE, None), P(TILE, None))
    return jax.shard_map(step, mesh=split, in_specs=in_specs, out_specs=out_specs, check_vma=False)
```

```python
import math

import jax
import jax.numpy as jnp
from jax import lax
from jax.experimental import pallas as pl
from jax.experimental.pallas import tpu as pltpu
from jax.sharding import Mesh
from jax.sharding import PartitionSpec as P

D = 512
FF = 1024
H = 512
NOISE = 128
NBRS = 8
HALO = 64
REGIONS = 8
MEMBERS = 8
CELLS = 512
BLOCK = CELLS // MEMBERS
CELLS_ALL = 32768
TILES = 64
HALF = D // 2
XY = TILES // 2
SHARE = 40
LOSS_ROW = 36

MEMBER = ("member_0", "core")
TILE = ("tile_0", "tile_1", "tile_2")
BF16 = jnp.bfloat16
F32 = jnp.float32


def counts(picks, start, rows, width):
    lanes = lax.broadcasted_iota(jnp.int32, (rows, width), 1) + start
    count = jnp.zeros((rows, width), F32)
    for k in range(NBRS):
        count = count + jnp.where(picks[:, k : k + 1] == lanes, 1.0 / NBRS, 0.0)
    return count.astype(BF16)


def teach(state, gathered, msg, up, down, loads=()):
    waits = [load.wait for load in loads] or [lambda: None] * 3
    waits[0]()
    resid = state.astype(F32) + jnp.dot(gathered, msg[...], preferred_element_type=F32)
    power = jnp.mean(resid * resid, axis=1, keepdims=True)
    normed = (resid * lax.rsqrt(power + 1e-06)).astype(BF16)
    waits[1]()
    hidden = jax.nn.silu(jnp.dot(normed, up[...], preferred_element_type=F32)).astype(BF16)
    waits[2]()
    return (resid + jnp.dot(hidden, down[...], preferred_element_type=F32)).astype(BF16)


def middle_kernel(
    state,
    noise,
    near,
    msg_at,
    up_at,
    down_at,
    out,
    sent,
    msg,
    up,
    down,
    held,
    sem,
    out_sem,
    noise_sem,
):
    loads = [
        pltpu.make_async_copy(source, target, sem.at[k])
        for k, (source, target) in enumerate(((msg_at, msg), (up_at, up), (down_at, down)))
    ]
    for copy in loads:
        copy.start()
    beside = pltpu.make_async_copy(noise, sent.at[:, D:], noise_sem)
    beside.start()
    sub = 128
    parts = []
    for at in range(0, CELLS - 2 * HALO, sub):
        picks = near[:, HALO + at : HALO + at + sub].T
        parts.append(
            jnp.dot(
                counts(picks, HALO + at, sub, 2 * sub),
                state[at : at + 2 * sub],
                preferred_element_type=F32,
            ).astype(BF16)
        )
    half = (CELLS - 2 * HALO) // 2
    gathered = jnp.concatenate(parts, axis=0)
    writes = []
    for k, at in enumerate((0, half)):
        held[at : at + half] = teach(
            state[HALO + at : HALO + at + half],
            gathered[at : at + half],
            msg,
            up,
            down,
            loads if k == 0 else (),
        )
        rows = pl.ds(HALO + at, half)
        for target, wait in ((out.at[rows], 2 * k), (sent.at[rows, :D], 2 * k + 1)):
            writes.append(
                pltpu.make_async_copy(held.at[at : at + half], target, out_sem.at[wait])
            )
            writes[-1].start()
    beside.wait()
    for copy in writes:
        copy.wait()


def edges_kernel(
    odd_swap,
    even_swap,
    state,
    near,
    msg,
    up,
    down,
    partly,
    partly_sent,
    odd,
    out,
    sent,
    held,
    sem,
):
    reach = 3 * HALO
    is_odd = jnp.full((HALO, D), odd[0], jnp.int32) == 1
    after_odd = odd_swap[...].astype(F32)
    after_even = even_swap[...].astype(F32)
    top = jnp.where(is_odd, after_even, after_odd).astype(BF16)
    bottom = jnp.where(is_odd, after_odd, after_even).astype(BF16)
    above = jnp.concatenate([top, state[: 2 * HALO]], axis=0)
    below = jnp.concatenate([state[CELLS - 2 * HALO :], bottom], axis=0)
    first = near[:, : 2 * HALO].T[:HALO]
    last = near[:, CELLS - 2 * HALO :].T[HALO:]
    gathered = jnp.concatenate(
        [
            jnp.dot(counts(first, 0, HALO, reach), above, preferred_element_type=F32),
            jnp.dot(
                counts(last, CELLS - HALO, HALO, reach), below, preferred_element_type=F32
            ),
        ],
        axis=0,
    ).astype(BF16)
    ends = jnp.concatenate([state[:HALO], state[CELLS - HALO :]], axis=0)
    held[...] = teach(ends, gathered, msg, up, down)
    writes = [
        pltpu.make_async_copy(held.at[:HALO], out.at[:HALO], sem.at[0]),
        pltpu.make_async_copy(held.at[HALO:], out.at[CELLS - HALO :], sem.at[1]),
        pltpu.make_async_copy(held.at[:HALO], sent.at[:HALO, :D], sem.at[2]),
        pltpu.make_async_copy(held.at[HALO:], sent.at[CELLS - HALO :, :D], sem.at[3]),
    ]
    for copy in writes:
        copy.start()
    for copy in writes:
        copy.wait()


def student_kernel(mine, w_in, w_out, early, turned, w_out_near):
    w_out_near[...] = w_out[...]
    rows = 256
    for at in range(0, CELLS, rows):
        state = mine[at : at + rows]
        early[at : at + rows] = jnp.dot(state, w_in[...], preferred_element_type=F32)
        turned[:, at : at + rows] = state.T


def score_kernel(
    early,
    mine,
    every,
    w_noise,
    w_out,
    turned,
    place,
    send,
    gst,
    gpre,
    turned_noise,
    shidden,
    loss_rows,
    wide,
    slope,
    student,
):
    rows = 256
    for at in range(0, CELLS, rows):
        draws = every[at // BLOCK : (at + rows) // BLOCK, :, D:].reshape(rows, NOISE)
        preact = early[at : at + rows] + jnp.dot(
            draws, w_noise[...], preferred_element_type=F32
        )
        sig = jax.nn.sigmoid(preact)
        hid = (preact * sig).astype(BF16)
        slope[at : at + rows] = sig * (1.0 + preact * (1.0 - sig))
        student[at : at + rows] = (
            mine[at : at + rows].astype(F32)
            + jnp.dot(hid, w_out[...], preferred_element_type=F32)
        ).astype(BF16)
        shidden[:, at : at + rows] = hid.T
        turned_noise[:, at : at + rows] = draws.T

    step = 16
    wide[...] = jnp.zeros_like(wide)

    def block(cell, lane):
        s = [
            student[pl.ds(cell + m * BLOCK, step), lane : lane + 128].astype(F32)
            for m in range(MEMBERS)
        ]
        g = [jnp.zeros((step, 128), F32) for _ in range(MEMBERS)]
        loss = jnp.zeros((step, 128), F32)
        for n in range(MEMBERS):
            t = every[n, pl.ds(cell, step), lane : lane + 128].astype(F32)
            for m in range(MEMBERS):
                d = s[m] - t
                q = d * d + 0.01
                inv = lax.rsqrt(q)
                loss = loss + q * inv
                g[m] = g[m] + d * inv
        ratio = (MEMBERS - 1) / MEMBERS
        loss = loss * ratio
        g = [x * ratio for x in g]
        for m in range(MEMBERS):
            for n in range(m + 1, MEMBERS):
                d = s[m] - s[n]
                q = d * d + 0.01
                inv = lax.rsqrt(q)
                r = d * inv
                loss = loss - q * inv
                g[m] = g[m] - r
                g[n] = g[n] + r
        scale = 1.0 / (MEMBERS * (MEMBERS - 1) * math.sqrt(CELLS_ALL))
        for m in range(MEMBERS):
            gst[m, pl.ds(cell, step), lane : lane + 128] = (g[m] * scale).astype(BF16)
        pairs = MEMBERS * (MEMBERS - 1)
        wide[...] += (loss - 0.1 * (pairs - pairs // 2)) * (1.0 / pairs)

    def body(i, carry):
        cell = pl.multiple_of(i * step, step)
        for lane in range(0, D, 128):
            block(cell, lane)
        return carry

    lax.fori_loop(0, BLOCK // step, body, 0)

    total = jnp.sum(jnp.sum(wide[...], axis=0, keepdims=True), axis=1, keepdims=True)
    lane_ids = lax.broadcasted_iota(jnp.int32, (4, 128), 1)
    at = jnp.where(lax.broadcasted_iota(jnp.int32, (4, 128), 0) == place[1], place[0], -128)
    spread = jnp.zeros((4, 128), F32)
    for k, piece in enumerate(three(total)):
        spread = spread + jnp.where(lane_ids == at + k * REGIONS, piece, 0.0)
    back = gst[...].reshape(CELLS, D)
    pull = lax.dot_general(
        back, w_out[...], (((1,), (1,)), ((), ())), preferred_element_type=F32
    )
    gpre[...] = (pull * slope[...]).astype(BF16)
    theirs = pl.multiple_of(jnp.where(place[1] == 0, HALF, 0), HALF)
    half_of_grads(theirs, turned, turned_noise, shidden, gst, gpre, spread, send)
    loss_rows[...] = spread


def half_of_grads(left, turned, turned_noise, shidden, gst, gpre, spread, target):
    spread = jnp.broadcast_to(spread[None], (XY, 4, 128))
    d_out = jnp.dot(
        shidden[...],
        gst[:, :, pl.ds(left, HALF)].reshape(CELLS, HALF),
        preferred_element_type=F32,
    )
    pulled = gpre[:, pl.ds(left, HALF)]
    d_in = jnp.dot(turned[...], pulled, preferred_element_type=F32)
    d_noise = jnp.dot(turned_noise[...], pulled, preferred_element_type=F32)
    for high in range(2):
        pieces = []
        for source, count in ((d_in, 8), (d_out, 8), (d_noise, 2)):
            start = high * XY * count
            for lane in (0, 128):
                pieces.append(
                    source[start : start + XY * count, lane : lane + 128].reshape(XY, count, 128)
                )
        pieces.append(spread)
        target[:, high] = jnp.concatenate(pieces, axis=1).astype(BF16)


def keep_kernel(turned, turned_noise, shidden, gst, gpre, loss_rows, place, keep):
    ours = pl.multiple_of(jnp.where(place[1] == 0, 0, HALF), HALF)
    half_of_grads(ours, turned, turned_noise, shidden, gst, gpre, loss_rows[...], keep)


def three(value):
    high = value.astype(BF16).astype(F32)
    middle = (value - high).astype(BF16).astype(F32)
    return high, middle, (value - high - middle).astype(BF16).astype(F32)


def fold_kernel(arrived, out):
    lanes = lax.broadcasted_iota(jnp.int32, (4, 128), 1)
    first = lax.broadcasted_iota(jnp.int32, (4, 128), 0) == 0
    for high in range(2):
        total = jnp.zeros((SHARE, 128), F32)
        for k in range(XY):
            total = total + arrived[k, high].astype(F32)
        tail = total[LOSS_ROW:]
        row = jnp.sum(tail, axis=0, keepdims=True)
        loss = row[:, :REGIONS] + row[:, REGIONS : 2 * REGIONS] + row[:, 2 * REGIONS : 3 * REGIONS]
        again = jnp.concatenate(
            [*three(loss), jnp.zeros((1, 128 - 3 * REGIONS), F32)], axis=1
        )
        share = jnp.concatenate(
            [total[:LOSS_ROW], jnp.where(first, again, jnp.zeros_like(tail))], axis=0
        ).astype(BF16)
        for k in range(MEMBERS):
            out[high * MEMBERS + k] = share


def last_kernel(arrived, region_loss, grad_in, grad_noise, grad_out):
    for half in range(2):
        total = arrived[half].astype(F32)
        for k in range(1, MEMBERS):
            total = total + arrived[2 * k + half].astype(F32)
        for part in range(2):
            left = half * HALF + part * 128
            grad_in[:, left : left + 128] = total[8 * part : 8 * part + 8]
            grad_out[:, left : left + 128] = total[16 + 8 * part : 24 + 8 * part]
            grad_noise[:, left : left + 128] = total[32 + 2 * part : 34 + 2 * part]
        if half == 0:
            row = total[LOSS_ROW : LOSS_ROW + 1]
            loss = (
                row[:, :REGIONS]
                + row[:, REGIONS : 2 * REGIONS]
                + row[:, 2 * REGIONS : 3 * REGIONS]
            )
            region_loss[...] = loss * (1.0 / (CELLS_ALL // REGIONS * D))


def exchanged(state, odd, first):
    ahead = odd if first else 1 - odd
    edge = lax.dynamic_slice_in_dim(state, ahead * (CELLS - HALO), HALO, axis=0)
    pairs = [(i, i + 1) for i in range(first, TILES - 1, 2)]
    return lax.ppermute(edge, TILE, pairs + [(b, a) for a, b in pairs])


HBM = pl.BlockSpec(memory_space=pltpu.HBM)
VMEM = pl.BlockSpec(memory_space=pltpu.VMEM)
PARAMS = pltpu.CompilerParams(vmem_limit_bytes=16 * 1024 * 1024)


def in_hbm(array):
    return pltpu.with_memory_space_constraint(array, pltpu.HBM)


def step(
    inputs,
    noise,
    neighbours,
    region_map,
    msg_weight,
    up_weight,
    down_weight,
    student_in,
    student_noise,
    student_out,
):
    state = inputs[0]
    mine = lax.all_to_all(
        state.reshape(MEMBERS, BLOCK, D), MEMBER, split_axis=0, concat_axis=0, tiled=True
    )
    odd = lax.axis_index("tile_2") % 2
    far = exchanged(state, odd, 1)
    near = exchanged(state, odd, 0)
    shapes = (
        jax.ShapeDtypeStruct((CELLS, D), BF16),
        jax.ShapeDtypeStruct((CELLS, D + NOISE), BF16),
    )
    middle = pl.pallas_call(
        middle_kernel,
        out_shape=shapes,
        in_specs=[VMEM] * 3 + [HBM] * 3,
        out_specs=[HBM] * 2,
        scratch_shapes=[
            pltpu.VMEM((D, D), BF16),
            pltpu.VMEM((D, FF), BF16),
            pltpu.VMEM((FF, D), BF16),
            pltpu.VMEM((CELLS - 2 * HALO, D), BF16),
            pltpu.SemaphoreType.DMA((3,)),
            pltpu.SemaphoreType.DMA((4,)),
            pltpu.SemaphoreType.DMA,
        ],
        compiler_params=PARAMS,
        name="middle",
    )
    edges = pl.pallas_call(
        edges_kernel,
        out_shape=shapes,
        in_specs=[VMEM] * 7 + [HBM] * 2 + [pl.BlockSpec(memory_space=pltpu.SMEM)],
        out_specs=[HBM] * 2,
        input_output_aliases={7: 0, 8: 1},
        scratch_shapes=[pltpu.VMEM((2 * HALO, D), BF16), pltpu.SemaphoreType.DMA((4,))],
        compiler_params=PARAMS,
        name="edges",
    )
    partly, partly_sent = middle(
        state,
        noise[0],
        neighbours,
        in_hbm(msg_weight),
        in_hbm(up_weight),
        in_hbm(down_weight),
    )
    teacher, sent = edges(
        far,
        near,
        state,
        neighbours,
        msg_weight,
        up_weight,
        down_weight,
        partly,
        partly_sent,
        odd.astype(jnp.int32).reshape(1),
    )
    every = lax.all_to_all(
        sent.reshape(MEMBERS, BLOCK, D + NOISE),
        MEMBER,
        split_axis=0,
        concat_axis=0,
        tiled=True,
    )
    mine = mine.reshape(CELLS, D)
    pupil = pl.pallas_call(
        student_kernel,
        out_shape=(
            jax.ShapeDtypeStruct((CELLS, H), F32),
            jax.ShapeDtypeStruct((D, CELLS), BF16),
            jax.ShapeDtypeStruct((H, D), BF16),
        ),
        in_specs=[VMEM] * 3,
        out_specs=[VMEM] * 3,
        compiler_params=PARAMS,
        name="student",
    )
    early, turned, w_out_near = pupil(mine, student_in, student_out)
    place = jnp.stack([region_map[0], lax.axis_index("core").astype(jnp.int32)])
    send, gst, gpre, turned_noise, shidden, loss_rows = pl.pallas_call(
        score_kernel,
        out_shape=[
            jax.ShapeDtypeStruct((XY, 2, SHARE, 128), BF16),
            jax.ShapeDtypeStruct((MEMBERS, BLOCK, D), BF16),
            jax.ShapeDtypeStruct((CELLS, D), BF16),
            jax.ShapeDtypeStruct((NOISE, CELLS), BF16),
            jax.ShapeDtypeStruct((H, CELLS), BF16),
            jax.ShapeDtypeStruct((4, 128), F32),
        ],
        in_specs=[VMEM] * 6 + [pl.BlockSpec(memory_space=pltpu.SMEM)],
        out_specs=[VMEM] * 6,
        scratch_shapes=[
            pltpu.VMEM((16, 128), F32),
            pltpu.VMEM((CELLS, H), F32),
            pltpu.VMEM((CELLS, D), BF16),
        ],
        compiler_params=PARAMS,
        name="score",
    )(early, mine, every, student_noise, w_out_near, turned, place)
    keep = pl.pallas_call(
        keep_kernel,
        out_shape=jax.ShapeDtypeStruct((XY, 2, SHARE, 128), BF16),
        in_specs=[VMEM] * 6 + [pl.BlockSpec(memory_space=pltpu.SMEM)],
        out_specs=VMEM,
        compiler_params=PARAMS,
        name="keep",
    )(turned, turned_noise, shidden, gst, gpre, loss_rows, place)
    other = lax.ppermute(send, "core", [(0, 1), (1, 0)])
    half = (keep.astype(F32) + other.astype(F32)).astype(BF16)
    shares = lax.all_to_all(half, ("tile_1", "tile_2"), split_axis=0, concat_axis=0, tiled=True)
    copies = pl.pallas_call(
        fold_kernel,
        out_shape=jax.ShapeDtypeStruct((2 * MEMBERS, SHARE, 128), BF16),
        in_specs=[VMEM],
        out_specs=VMEM,
        compiler_params=PARAMS,
        name="fold",
    )(shares)
    parts = lax.all_to_all(
        copies, ("tile_0", "member_0", "core"), split_axis=0, concat_axis=0, tiled=True
    )
    region_loss, grad_in, grad_noise, grad_out = pl.pallas_call(
        last_kernel,
        out_shape=[
            jax.ShapeDtypeStruct((1, REGIONS), F32),
            jax.ShapeDtypeStruct((8, D), F32),
            jax.ShapeDtypeStruct((2, D), F32),
            jax.ShapeDtypeStruct((8, D), F32),
        ],
        in_specs=[VMEM],
        out_specs=[VMEM] * 4,
        compiler_params=PARAMS,
        name="last",
    )(parts)
    return (teacher[None], region_loss.reshape(REGIONS), grad_in, grad_noise, grad_out)


def solution(mesh):
    split = Mesh(
        mesh.devices.reshape(4, 2, 2, 4, 8), ("member_0", "core", "tile_0", "tile_1", "tile_2")
    )
    in_specs = (
        P(MEMBER, TILE, None),
        P(MEMBER, TILE, None),
        P(None, TILE),
        P(TILE),
        P(),
        P(),
        P(),
        P(),
        P(),
        P(),
    )
    out_specs = (P(MEMBER, TILE, None), P(), P(TILE, None), P(TILE, None), P(TILE, None))
    return jax.shard_map(step, mesh=split, in_specs=in_specs, out_specs=out_specs, check_vma=False)
```

```python
import math

import jax
import jax.numpy as jnp
from jax import lax
from jax.experimental import pallas as pl
from jax.experimental.pallas import tpu as pltpu
from jax.sharding import Mesh
from jax.sharding import PartitionSpec as P

D = 512
FF = 1024
H = 512
NOISE = 128
NBRS = 8
HALO = 64
REGIONS = 8
MEMBERS = 8
CELLS = 512
BLOCK = CELLS // MEMBERS
CELLS_ALL = 32768
TILES = 64
HALF = D // 2
XY = TILES // 2
SHARE = 40
LOSS_ROW = 36

MEMBER = ("member_0", "core")
TILE = ("tile_0", "tile_1", "tile_2")
BF16 = jnp.bfloat16
F32 = jnp.float32


def counts(picks, start, rows, width):
    lanes = lax.broadcasted_iota(jnp.int32, (rows, width), 1) + start
    count = jnp.zeros((rows, width), F32)
    for k in range(NBRS):
        count = count + jnp.where(picks[:, k : k + 1] == lanes, 1.0 / NBRS, 0.0)
    return count.astype(BF16)


def teach(state, gathered, msg, up, down, loads=()):
    waits = [load.wait for load in loads] or [lambda: None] * 3
    waits[0]()
    resid = state.astype(F32) + jnp.dot(gathered, msg[...], preferred_element_type=F32)
    power = jnp.mean(resid * resid, axis=1, keepdims=True)
    normed = (resid * lax.rsqrt(power + 1e-06)).astype(BF16)
    waits[1]()
    hidden = jax.nn.silu(jnp.dot(normed, up[...], preferred_element_type=F32)).astype(BF16)
    waits[2]()
    return (resid + jnp.dot(hidden, down[...], preferred_element_type=F32)).astype(BF16)


def middle_kernel(
    state,
    noise,
    near,
    msg_at,
    up_at,
    down_at,
    out,
    sent,
    msg,
    up,
    down,
    held,
    sem,
    out_sem,
    noise_sem,
):
    loads = [
        pltpu.make_async_copy(source, target, sem.at[k])
        for k, (source, target) in enumerate(((msg_at, msg), (up_at, up), (down_at, down)))
    ]
    for copy in loads:
        copy.start()
    beside = pltpu.make_async_copy(noise, sent.at[:, D:], noise_sem)
    beside.start()
    sub = 128
    parts = []
    for at in range(0, CELLS - 2 * HALO, sub):
        picks = near[:, HALO + at : HALO + at + sub].T
        parts.append(
            jnp.dot(
                counts(picks, HALO + at, sub, 2 * sub),
                state[at : at + 2 * sub],
                preferred_element_type=F32,
            ).astype(BF16)
        )
    half = (CELLS - 2 * HALO) // 2
    gathered = jnp.concatenate(parts, axis=0)
    writes = []
    for k, at in enumerate((0, half)):
        held[at : at + half] = teach(
            state[HALO + at : HALO + at + half],
            gathered[at : at + half],
            msg,
            up,
            down,
            loads if k == 0 else (),
        )
        rows = pl.ds(HALO + at, half)
        for target, wait in ((out.at[rows], 2 * k), (sent.at[rows, :D], 2 * k + 1)):
            writes.append(
                pltpu.make_async_copy(held.at[at : at + half], target, out_sem.at[wait])
            )
            writes[-1].start()
    beside.wait()
    for copy in writes:
        copy.wait()


def edges_kernel(
    odd_swap,
    even_swap,
    state,
    near,
    msg,
    up,
    down,
    partly,
    partly_sent,
    odd,
    out,
    sent,
    held,
    sem,
):
    reach = 3 * HALO
    is_odd = jnp.full((HALO, D), odd[0], jnp.int32) == 1
    after_odd = odd_swap[...].astype(F32)
    after_even = even_swap[...].astype(F32)
    top = jnp.where(is_odd, after_even, after_odd).astype(BF16)
    bottom = jnp.where(is_odd, after_odd, after_even).astype(BF16)
    above = jnp.concatenate([top, state[: 2 * HALO]], axis=0)
    below = jnp.concatenate([state[CELLS - 2 * HALO :], bottom], axis=0)
    first = near[:, : 2 * HALO].T[:HALO]
    last = near[:, CELLS - 2 * HALO :].T[HALO:]
    gathered = jnp.concatenate(
        [
            jnp.dot(counts(first, 0, HALO, reach), above, preferred_element_type=F32),
            jnp.dot(
                counts(last, CELLS - HALO, HALO, reach), below, preferred_element_type=F32
            ),
        ],
        axis=0,
    ).astype(BF16)
    ends = jnp.concatenate([state[:HALO], state[CELLS - HALO :]], axis=0)
    held[...] = teach(ends, gathered, msg, up, down)
    writes = [
        pltpu.make_async_copy(held.at[:HALO], out.at[:HALO], sem.at[0]),
        pltpu.make_async_copy(held.at[HALO:], out.at[CELLS - HALO :], sem.at[1]),
        pltpu.make_async_copy(held.at[:HALO], sent.at[:HALO, :D], sem.at[2]),
        pltpu.make_async_copy(held.at[HALO:], sent.at[CELLS - HALO :, :D], sem.at[3]),
    ]
    for copy in writes:
        copy.start()
    for copy in writes:
        copy.wait()


def student_kernel(mine, w_in, early, turned):
    rows = 256
    for at in range(0, CELLS, rows):
        state = mine[at : at + rows]
        early[at : at + rows] = jnp.dot(state, w_in[...], preferred_element_type=F32)
        turned[:, at : at + rows] = state.T


def score_kernel(
    early,
    mine,
    every,
    w_noise,
    w_out_at,
    turned_at,
    place,
    send,
    gst,
    gpre,
    turned,
    turned_noise,
    shidden,
    loss_rows,
    wide,
    slope,
    student,
    hidden,
    w_out,
    sem,
):
    copies = [
        pltpu.make_async_copy(w_out_at, w_out, sem.at[0]),
        pltpu.make_async_copy(turned_at, turned, sem.at[1]),
    ]
    for copy in copies:
        copy.start()
    rows = 256
    for at in range(0, CELLS, rows):
        draws = every[at // BLOCK : (at + rows) // BLOCK, :, D:].reshape(rows, NOISE)
        preact = early[at : at + rows] + jnp.dot(
            draws, w_noise[...], preferred_element_type=F32
        )
        sig = jax.nn.sigmoid(preact)
        hid = (preact * sig).astype(BF16)
        hidden[at : at + rows] = hid
        slope[at : at + rows] = sig * (1.0 + preact * (1.0 - sig))
        shidden[:, at : at + rows] = hid.T
        turned_noise[:, at : at + rows] = draws.T
    copies[0].wait()
    for at in range(0, CELLS, rows):
        student[at : at + rows] = (
            mine[at : at + rows].astype(F32)
            + jnp.dot(hidden[at : at + rows], w_out[...], preferred_element_type=F32)
        ).astype(BF16)

    step = 16
    wide[...] = jnp.zeros_like(wide)

    def block(cell, lane):
        s = [
            student[pl.ds(cell + m * BLOCK, step), lane : lane + 128].astype(F32)
            for m in range(MEMBERS)
        ]
        g = [jnp.zeros((step, 128), F32) for _ in range(MEMBERS)]
        loss = jnp.zeros((step, 128), F32)
        for n in range(MEMBERS):
            t = every[n, pl.ds(cell, step), lane : lane + 128].astype(F32)
            for m in range(MEMBERS):
                d = s[m] - t
                q = d * d + 0.01
                inv = lax.rsqrt(q)
                loss = loss + q * inv
                g[m] = g[m] + d * inv
        ratio = (MEMBERS - 1) / MEMBERS
        loss = loss * ratio
        g = [x * ratio for x in g]
        for m in range(MEMBERS):
            for n in range(m + 1, MEMBERS):
                d = s[m] - s[n]
                q = d * d + 0.01
                inv = lax.rsqrt(q)
                r = d * inv
                loss = loss - q * inv
                g[m] = g[m] - r
                g[n] = g[n] + r
        scale = 1.0 / (MEMBERS * (MEMBERS - 1) * math.sqrt(CELLS_ALL))
        for m in range(MEMBERS):
            gst[m, pl.ds(cell, step), lane : lane + 128] = (g[m] * scale).astype(BF16)
        pairs = MEMBERS * (MEMBERS - 1)
        wide[...] += (loss - 0.1 * (pairs - pairs // 2)) * (1.0 / pairs)

    def body(i, carry):
        cell = pl.multiple_of(i * step, step)
        for lane in range(0, D, 128):
            block(cell, lane)
        return carry

    lax.fori_loop(0, BLOCK // step, body, 0)

    total = jnp.sum(jnp.sum(wide[...], axis=0, keepdims=True), axis=1, keepdims=True)
    lane_ids = lax.broadcasted_iota(jnp.int32, (4, 128), 1)
    at = jnp.where(lax.broadcasted_iota(jnp.int32, (4, 128), 0) == place[1], place[0], -128)
    spread = jnp.zeros((4, 128), F32)
    for k, piece in enumerate(three(total)):
        spread = spread + jnp.where(lane_ids == at + k * REGIONS, piece, 0.0)
    copies[1].wait()
    back = gst[...].reshape(CELLS, D)
    pull = lax.dot_general(
        back, w_out[...], (((1,), (1,)), ((), ())), preferred_element_type=F32
    )
    gpre[...] = (pull * slope[...]).astype(BF16)
    theirs = pl.multiple_of(jnp.where(place[1] == 0, HALF, 0), HALF)
    half_of_grads(theirs, turned, turned_noise, shidden, gst, gpre, spread, send)
    loss_rows[...] = spread


def half_of_grads(left, turned, turned_noise, shidden, gst, gpre, spread, target):
    spread = jnp.broadcast_to(spread[None], (XY, 4, 128))
    d_out = jnp.dot(
        shidden[...],
        gst[:, :, pl.ds(left, HALF)].reshape(CELLS, HALF),
        preferred_element_type=F32,
    )
    pulled = gpre[:, pl.ds(left, HALF)]
    d_in = jnp.dot(turned[...], pulled, preferred_element_type=F32)
    d_noise = jnp.dot(turned_noise[...], pulled, preferred_element_type=F32)
    for high in range(2):
        pieces = []
        for source, count in ((d_in, 8), (d_out, 8), (d_noise, 2)):
            start = high * XY * count
            for lane in (0, 128):
                pieces.append(
                    source[start : start + XY * count, lane : lane + 128].reshape(XY, count, 128)
                )
        pieces.append(spread)
        target[:, high] = jnp.concatenate(pieces, axis=1).astype(BF16)


def keep_kernel(turned, turned_noise, shidden, gst, gpre, loss_rows, place, keep):
    ours = pl.multiple_of(jnp.where(place[1] == 0, 0, HALF), HALF)
    half_of_grads(ours, turned, turned_noise, shidden, gst, gpre, loss_rows[...], keep)


def three(value):
    high = value.astype(BF16).astype(F32)
    middle = (value - high).astype(BF16).astype(F32)
    return high, middle, (value - high - middle).astype(BF16).astype(F32)


def fold_kernel(arrived, out):
    lanes = lax.broadcasted_iota(jnp.int32, (4, 128), 1)
    first = lax.broadcasted_iota(jnp.int32, (4, 128), 0) == 0
    for high in range(2):
        total = jnp.zeros((SHARE, 128), F32)
        for k in range(XY):
            total = total + arrived[k, high].astype(F32)
        tail = total[LOSS_ROW:]
        row = jnp.sum(tail, axis=0, keepdims=True)
        loss = row[:, :REGIONS] + row[:, REGIONS : 2 * REGIONS] + row[:, 2 * REGIONS : 3 * REGIONS]
        again = jnp.concatenate(
            [*three(loss), jnp.zeros((1, 128 - 3 * REGIONS), F32)], axis=1
        )
        share = jnp.concatenate(
            [total[:LOSS_ROW], jnp.where(first, again, jnp.zeros_like(tail))], axis=0
        ).astype(BF16)
        for k in range(MEMBERS):
            out[high * MEMBERS + k] = share


def last_kernel(arrived, region_loss, grad_in, grad_noise, grad_out):
    for half in range(2):
        total = arrived[half].astype(F32)
        for k in range(1, MEMBERS):
            total = total + arrived[2 * k + half].astype(F32)
        for part in range(2):
            left = half * HALF + part * 128
            grad_in[:, left : left + 128] = total[8 * part : 8 * part + 8]
            grad_out[:, left : left + 128] = total[16 + 8 * part : 24 + 8 * part]
            grad_noise[:, left : left + 128] = total[32 + 2 * part : 34 + 2 * part]
        if half == 0:
            row = total[LOSS_ROW : LOSS_ROW + 1]
            loss = (
                row[:, :REGIONS]
                + row[:, REGIONS : 2 * REGIONS]
                + row[:, 2 * REGIONS : 3 * REGIONS]
            )
            region_loss[...] = loss * (1.0 / (CELLS_ALL // REGIONS * D))


def exchanged(state, odd, first):
    ahead = odd if first else 1 - odd
    edge = lax.dynamic_slice_in_dim(state, ahead * (CELLS - HALO), HALO, axis=0)
    pairs = [(i, i + 1) for i in range(first, TILES - 1, 2)]
    return lax.ppermute(edge, TILE, pairs + [(b, a) for a, b in pairs])


HBM = pl.BlockSpec(memory_space=pltpu.HBM)
VMEM = pl.BlockSpec(memory_space=pltpu.VMEM)
PARAMS = pltpu.CompilerParams(vmem_limit_bytes=16 * 1024 * 1024)


def in_hbm(array):
    return pltpu.with_memory_space_constraint(array, pltpu.HBM)


def step(
    inputs,
    noise,
    neighbours,
    region_map,
    msg_weight,
    up_weight,
    down_weight,
    student_in,
    student_noise,
    student_out,
):
    state = inputs[0]
    mine = lax.all_to_all(
        state.reshape(MEMBERS, BLOCK, D), MEMBER, split_axis=0, concat_axis=0, tiled=True
    )
    odd = lax.axis_index("tile_2") % 2
    far = exchanged(state, odd, 1)
    near = exchanged(state, odd, 0)
    shapes = (
        jax.ShapeDtypeStruct((CELLS, D), BF16),
        jax.ShapeDtypeStruct((CELLS, D + NOISE), BF16),
    )
    middle = pl.pallas_call(
        middle_kernel,
        out_shape=shapes,
        in_specs=[VMEM] * 3 + [HBM] * 3,
        out_specs=[HBM] * 2,
        scratch_shapes=[
            pltpu.VMEM((D, D), BF16),
            pltpu.VMEM((D, FF), BF16),
            pltpu.VMEM((FF, D), BF16),
            pltpu.VMEM((CELLS - 2 * HALO, D), BF16),
            pltpu.SemaphoreType.DMA((3,)),
            pltpu.SemaphoreType.DMA((4,)),
            pltpu.SemaphoreType.DMA,
        ],
        compiler_params=PARAMS,
        name="middle",
    )
    edges = pl.pallas_call(
        edges_kernel,
        out_shape=shapes,
        in_specs=[VMEM] * 7 + [HBM] * 2 + [pl.BlockSpec(memory_space=pltpu.SMEM)],
        out_specs=[HBM] * 2,
        input_output_aliases={7: 0, 8: 1},
        scratch_shapes=[pltpu.VMEM((2 * HALO, D), BF16), pltpu.SemaphoreType.DMA((4,))],
        compiler_params=PARAMS,
        name="edges",
    )
    partly, partly_sent = middle(
        state,
        noise[0],
        neighbours,
        in_hbm(msg_weight),
        in_hbm(up_weight),
        in_hbm(down_weight),
    )
    teacher, sent = edges(
        far,
        near,
        state,
        neighbours,
        msg_weight,
        up_weight,
        down_weight,
        partly,
        partly_sent,
        odd.astype(jnp.int32).reshape(1),
    )
    every = lax.all_to_all(
        sent.reshape(MEMBERS, BLOCK, D + NOISE),
        MEMBER,
        split_axis=0,
        concat_axis=0,
        tiled=True,
    )
    mine = mine.reshape(CELLS, D)
    pupil = pl.pallas_call(
        student_kernel,
        out_shape=(
            jax.ShapeDtypeStruct((CELLS, H), F32),
            jax.ShapeDtypeStruct((D, CELLS), BF16),
        ),
        in_specs=[VMEM] * 2,
        out_specs=[VMEM] * 2,
        compiler_params=PARAMS,
        name="student",
    )
    early, turned_far = pupil(mine, student_in)
    place = jnp.stack([region_map[0], lax.axis_index("core").astype(jnp.int32)])
    send, gst, gpre, turned, turned_noise, shidden, loss_rows = pl.pallas_call(
        score_kernel,
        out_shape=[
            jax.ShapeDtypeStruct((XY, 2, SHARE, 128), BF16),
            jax.ShapeDtypeStruct((MEMBERS, BLOCK, D), BF16),
            jax.ShapeDtypeStruct((CELLS, D), BF16),
            jax.ShapeDtypeStruct((D, CELLS), BF16),
            jax.ShapeDtypeStruct((NOISE, CELLS), BF16),
            jax.ShapeDtypeStruct((H, CELLS), BF16),
            jax.ShapeDtypeStruct((4, 128), F32),
        ],
        in_specs=[VMEM] * 4 + [HBM] * 2 + [pl.BlockSpec(memory_space=pltpu.SMEM)],
        out_specs=[VMEM] * 7,
        scratch_shapes=[
            pltpu.VMEM((16, 128), F32),
            pltpu.VMEM((CELLS, H), F32),
            pltpu.VMEM((CELLS, D), BF16),
            pltpu.VMEM((CELLS, H), BF16),
            pltpu.VMEM((H, D), BF16),
            pltpu.SemaphoreType.DMA((2,)),
        ],
        compiler_params=PARAMS,
        name="score",
    )(early, mine, every, student_noise, in_hbm(student_out), in_hbm(turned_far), place)
    keep = pl.pallas_call(
        keep_kernel,
        out_shape=jax.ShapeDtypeStruct((XY, 2, SHARE, 128), BF16),
        in_specs=[VMEM] * 6 + [pl.BlockSpec(memory_space=pltpu.SMEM)],
        out_specs=VMEM,
        compiler_params=PARAMS,
        name="keep",
    )(turned, turned_noise, shidden, gst, gpre, loss_rows, place)
    other = lax.ppermute(send, "core", [(0, 1), (1, 0)])
    half = (keep.astype(F32) + other.astype(F32)).astype(BF16)
    shares = lax.all_to_all(half, ("tile_1", "tile_2"), split_axis=0, concat_axis=0, tiled=True)
    copies = pl.pallas_call(
        fold_kernel,
        out_shape=jax.ShapeDtypeStruct((2 * MEMBERS, SHARE, 128), BF16),
        in_specs=[VMEM],
        out_specs=VMEM,
        compiler_params=PARAMS,
        name="fold",
    )(shares)
    parts = lax.all_to_all(
        copies, ("tile_0", "member_0", "core"), split_axis=0, concat_axis=0, tiled=True
    )
    region_loss, grad_in, grad_noise, grad_out = pl.pallas_call(
        last_kernel,
        out_shape=[
            jax.ShapeDtypeStruct((1, REGIONS), F32),
            jax.ShapeDtypeStruct((8, D), F32),
            jax.ShapeDtypeStruct((2, D), F32),
            jax.ShapeDtypeStruct((8, D), F32),
        ],
        in_specs=[VMEM],
        out_specs=[VMEM] * 4,
        compiler_params=PARAMS,
        name="last",
    )(parts)
    return (teacher[None], region_loss.reshape(REGIONS), grad_in, grad_noise, grad_out)


def solution(mesh):
    split = Mesh(
        mesh.devices.reshape(4, 2, 2, 4, 8), ("member_0", "core", "tile_0", "tile_1", "tile_2")
    )
    in_specs = (
        P(MEMBER, TILE, None),
        P(MEMBER, TILE, None),
        P(None, TILE),
        P(TILE),
        P(),
        P(),
        P(),
        P(),
        P(),
        P(),
    )
    out_specs = (P(MEMBER, TILE, None), P(), P(TILE, None), P(TILE, None), P(TILE, None))
    return jax.shard_map(step, mesh=split, in_specs=in_specs, out_specs=out_specs, check_vma=False)
```

```python
import math

import jax
import jax.numpy as jnp
from jax import lax
from jax.experimental import pallas as pl
from jax.experimental.pallas import tpu as pltpu
from jax.sharding import Mesh
from jax.sharding import PartitionSpec as P

D = 512
FF = 1024
H = 512
NOISE = 128
NBRS = 8
HALO = 64
REGIONS = 8
MEMBERS = 8
CELLS = 512
BLOCK = CELLS // MEMBERS
CELLS_ALL = 32768
TILES = 64
HALF = D // 2
XY = TILES // 2
SHARE = 40
LOSS_ROW = 36

MEMBER = ("member_0", "core")
TILE = ("tile_0", "tile_1", "tile_2")
BF16 = jnp.bfloat16
F32 = jnp.float32


def counts(picks, start, rows, width):
    lanes = lax.broadcasted_iota(jnp.int32, (rows, width), 1) + start
    count = jnp.zeros((rows, width), F32)
    for k in range(NBRS):
        count = count + jnp.where(picks[:, k : k + 1] == lanes, 1.0 / NBRS, 0.0)
    return count.astype(BF16)


def teach(state, gathered, msg, up, down, loads=()):
    waits = [load.wait for load in loads] or [lambda: None] * 3
    waits[0]()
    resid = state.astype(F32) + jnp.dot(gathered, msg[...], preferred_element_type=F32)
    power = jnp.mean(resid * resid, axis=1, keepdims=True)
    normed = (resid * lax.rsqrt(power + 1e-06)).astype(BF16)
    waits[1]()
    hidden = jax.nn.silu(jnp.dot(normed, up[...], preferred_element_type=F32)).astype(BF16)
    waits[2]()
    return (resid + jnp.dot(hidden, down[...], preferred_element_type=F32)).astype(BF16)


def middle_kernel(
    state,
    noise,
    near,
    msg_at,
    up_at,
    down_at,
    out,
    sent,
    msg,
    up,
    down,
    held,
    sem,
    out_sem,
    noise_sem,
):
    loads = [
        pltpu.make_async_copy(source, target, sem.at[k])
        for k, (source, target) in enumerate(((msg_at, msg), (up_at, up), (down_at, down)))
    ]
    for copy in loads:
        copy.start()
    beside = pltpu.make_async_copy(noise, sent.at[:, D:], noise_sem)
    beside.start()
    sub = 128
    parts = []
    for at in range(0, CELLS - 2 * HALO, sub):
        picks = near[:, HALO + at : HALO + at + sub].T
        parts.append(
            jnp.dot(
                counts(picks, HALO + at, sub, 2 * sub),
                state[at : at + 2 * sub],
                preferred_element_type=F32,
            ).astype(BF16)
        )
    half = (CELLS - 2 * HALO) // 2
    gathered = jnp.concatenate(parts, axis=0)
    writes = []
    for k, at in enumerate((0, half)):
        held[at : at + half] = teach(
            state[HALO + at : HALO + at + half],
            gathered[at : at + half],
            msg,
            up,
            down,
            loads if k == 0 else (),
        )
        rows = pl.ds(HALO + at, half)
        for target, wait in ((out.at[rows], 2 * k), (sent.at[rows, :D], 2 * k + 1)):
            writes.append(
                pltpu.make_async_copy(held.at[at : at + half], target, out_sem.at[wait])
            )
            writes[-1].start()
    beside.wait()
    for copy in writes:
        copy.wait()


def edges_kernel(
    odd_swap,
    even_swap,
    state,
    near,
    msg,
    up,
    down,
    partly,
    partly_sent,
    odd,
    out,
    sent,
    held,
    sem,
):
    reach = 3 * HALO
    is_odd = jnp.full((HALO, D), odd[0], jnp.int32) == 1
    after_odd = odd_swap[...].astype(F32)
    after_even = even_swap[...].astype(F32)
    top = jnp.where(is_odd, after_even, after_odd).astype(BF16)
    bottom = jnp.where(is_odd, after_odd, after_even).astype(BF16)
    above = jnp.concatenate([top, state[: 2 * HALO]], axis=0)
    below = jnp.concatenate([state[CELLS - 2 * HALO :], bottom], axis=0)
    first = near[:, : 2 * HALO].T[:HALO]
    last = near[:, CELLS - 2 * HALO :].T[HALO:]
    gathered = jnp.concatenate(
        [
            jnp.dot(counts(first, 0, HALO, reach), above, preferred_element_type=F32),
            jnp.dot(
                counts(last, CELLS - HALO, HALO, reach), below, preferred_element_type=F32
            ),
        ],
        axis=0,
    ).astype(BF16)
    ends = jnp.concatenate([state[:HALO], state[CELLS - HALO :]], axis=0)
    held[...] = teach(ends, gathered, msg, up, down)
    writes = [
        pltpu.make_async_copy(held.at[:HALO], out.at[:HALO], sem.at[0]),
        pltpu.make_async_copy(held.at[HALO:], out.at[CELLS - HALO :], sem.at[1]),
        pltpu.make_async_copy(held.at[:HALO], sent.at[:HALO, :D], sem.at[2]),
        pltpu.make_async_copy(held.at[HALO:], sent.at[CELLS - HALO :, :D], sem.at[3]),
    ]
    for copy in writes:
        copy.start()
    for copy in writes:
        copy.wait()


def student_kernel(mine, w_in, early, turned):
    rows = 256
    for at in range(0, CELLS, rows):
        state = mine[at : at + rows]
        early[at : at + rows] = jnp.dot(state, w_in[...], preferred_element_type=F32)
        turned[:, at : at + rows] = state.T


def score_kernel(
    early,
    mine,
    every,
    w_noise,
    w_out,
    turned_at,
    place,
    send,
    keep,
    gst,
    gpre,
    wide,
    turned,
    turned_noise,
    shidden,
    slope,
    student,
    sem,
):
    copy = pltpu.make_async_copy(turned_at, turned, sem)
    copy.start()
    rows = 256
    for at in range(0, CELLS, rows):
        draws = every[at // BLOCK : (at + rows) // BLOCK, :, D:].reshape(rows, NOISE)
        preact = early[at : at + rows] + jnp.dot(
            draws, w_noise[...], preferred_element_type=F32
        )
        sig = jax.nn.sigmoid(preact)
        hid = (preact * sig).astype(BF16)
        slope[at : at + rows] = sig * (1.0 + preact * (1.0 - sig))
        student[at : at + rows] = (
            mine[at : at + rows].astype(F32)
            + jnp.dot(hid, w_out[...], preferred_element_type=F32)
        ).astype(BF16)
        shidden[:, at : at + rows] = hid.T
        turned_noise[:, at : at + rows] = draws.T

    step = 16
    wide[...] = jnp.zeros_like(wide)

    def block(cell, lane):
        s = [
            student[pl.ds(cell + m * BLOCK, step), lane : lane + 128].astype(F32)
            for m in range(MEMBERS)
        ]
        g = [jnp.zeros((step, 128), F32) for _ in range(MEMBERS)]
        loss = jnp.zeros((step, 128), F32)
        for n in range(MEMBERS):
            t = every[n, pl.ds(cell, step), lane : lane + 128].astype(F32)
            for m in range(MEMBERS):
                d = s[m] - t
                q = d * d + 0.01
                inv = lax.rsqrt(q)
                loss = loss + q * inv
                g[m] = g[m] + d * inv
        ratio = (MEMBERS - 1) / MEMBERS
        loss = loss * ratio
        g = [x * ratio for x in g]
        for m in range(MEMBERS):
            for n in range(m + 1, MEMBERS):
                d = s[m] - s[n]
                q = d * d + 0.01
                inv = lax.rsqrt(q)
                r = d * inv
                loss = loss - q * inv
                g[m] = g[m] - r
                g[n] = g[n] + r
        scale = 1.0 / (MEMBERS * (MEMBERS - 1) * math.sqrt(CELLS_ALL))
        for m in range(MEMBERS):
            gst[m, pl.ds(cell, step), lane : lane + 128] = (g[m] * scale).astype(BF16)
        pairs = MEMBERS * (MEMBERS - 1)
        wide[...] += (loss - 0.1 * (pairs - pairs // 2)) * (1.0 / pairs)

    def body(i, carry):
        cell = pl.multiple_of(i * step, step)
        for lane in range(0, D, 128):
            block(cell, lane)
        return carry

    lax.fori_loop(0, BLOCK // step, body, 0)

    total = jnp.sum(jnp.sum(wide[...], axis=0, keepdims=True), axis=1, keepdims=True)
    lane_ids = lax.broadcasted_iota(jnp.int32, (4, 128), 1)
    at = jnp.where(lax.broadcasted_iota(jnp.int32, (4, 128), 0) == place[1], place[0], -128)
    spread = jnp.zeros((4, 128), F32)
    for k, piece in enumerate(three(total)):
        spread = spread + jnp.where(lane_ids == at + k * REGIONS, piece, 0.0)
    spread = jnp.broadcast_to(spread[None], (XY, 4, 128))

    copy.wait()
    back = gst[...].reshape(CELLS, D)
    pull = lax.dot_general(
        back, w_out[...], (((1,), (1,)), ((), ())), preferred_element_type=F32
    )
    gpre[...] = (pull * slope[...]).astype(BF16)
    for k, target in enumerate((send, keep)):
        left = pl.multiple_of(jnp.where(place[1] == k, HALF, 0), HALF)
        d_out = jnp.dot(
            shidden[...], gst[:, :, pl.ds(left, HALF)].reshape(CELLS, HALF), preferred_element_type=F32
        )
        pulled = gpre[:, pl.ds(left, HALF)]
        d_in = jnp.dot(turned[...], pulled, preferred_element_type=F32)
        d_noise = jnp.dot(turned_noise[...], pulled, preferred_element_type=F32)
        for high in range(2):
            pieces = []
            for source, count in ((d_in, 8), (d_out, 8), (d_noise, 2)):
                start = high * XY * count
                for lane in (0, 128):
                    pieces.append(
                        source[start : start + XY * count, lane : lane + 128].reshape(
                            XY, count, 128
                        )
                    )
            pieces.append(spread)
            target[:, high] = jnp.concatenate(pieces, axis=1).astype(BF16)


def three(value):
    high = value.astype(BF16).astype(F32)
    middle = (value - high).astype(BF16).astype(F32)
    return high, middle, (value - high - middle).astype(BF16).astype(F32)


def fold_kernel(arrived, out):
    lanes = lax.broadcasted_iota(jnp.int32, (4, 128), 1)
    first = lax.broadcasted_iota(jnp.int32, (4, 128), 0) == 0
    for high in range(2):
        total = jnp.zeros((SHARE, 128), F32)
        for k in range(XY):
            total = total + arrived[k, high].astype(F32)
        tail = total[LOSS_ROW:]
        row = jnp.sum(tail, axis=0, keepdims=True)
        loss = row[:, :REGIONS] + row[:, REGIONS : 2 * REGIONS] + row[:, 2 * REGIONS : 3 * REGIONS]
        again = jnp.concatenate(
            [*three(loss), jnp.zeros((1, 128 - 3 * REGIONS), F32)], axis=1
        )
        share = jnp.concatenate(
            [total[:LOSS_ROW], jnp.where(first, again, jnp.zeros_like(tail))], axis=0
        ).astype(BF16)
        for k in range(MEMBERS):
            out[high * MEMBERS + k] = share


def last_kernel(arrived, region_loss, grad_in, grad_noise, grad_out):
    for half in range(2):
        total = arrived[half].astype(F32)
        for k in range(1, MEMBERS):
            total = total + arrived[2 * k + half].astype(F32)
        for part in range(2):
            left = half * HALF + part * 128
            grad_in[:, left : left + 128] = total[8 * part : 8 * part + 8]
            grad_out[:, left : left + 128] = total[16 + 8 * part : 24 + 8 * part]
            grad_noise[:, left : left + 128] = total[32 + 2 * part : 34 + 2 * part]
        if half == 0:
            row = total[LOSS_ROW : LOSS_ROW + 1]
            loss = (
                row[:, :REGIONS]
                + row[:, REGIONS : 2 * REGIONS]
                + row[:, 2 * REGIONS : 3 * REGIONS]
            )
            region_loss[...] = loss * (1.0 / (CELLS_ALL // REGIONS * D))


def exchanged(state, odd, first):
    ahead = odd if first else 1 - odd
    edge = lax.dynamic_slice_in_dim(state, ahead * (CELLS - HALO), HALO, axis=0)
    pairs = [(i, i + 1) for i in range(first, TILES - 1, 2)]
    return lax.ppermute(edge, TILE, pairs + [(b, a) for a, b in pairs])


HBM = pl.BlockSpec(memory_space=pltpu.HBM)
VMEM = pl.BlockSpec(memory_space=pltpu.VMEM)
PARAMS = pltpu.CompilerParams(vmem_limit_bytes=16 * 1024 * 1024)


def in_hbm(array):
    return pltpu.with_memory_space_constraint(array, pltpu.HBM)


def step(
    inputs,
    noise,
    neighbours,
    region_map,
    msg_weight,
    up_weight,
    down_weight,
    student_in,
    student_noise,
    student_out,
):
    state = inputs[0]
    mine = lax.all_to_all(
        state.reshape(MEMBERS, BLOCK, D), MEMBER, split_axis=0, concat_axis=0, tiled=True
    )
    odd = lax.axis_index("tile_2") % 2
    far = exchanged(state, odd, 1)
    near = exchanged(state, odd, 0)
    shapes = (
        jax.ShapeDtypeStruct((CELLS, D), BF16),
        jax.ShapeDtypeStruct((CELLS, D + NOISE), BF16),
    )
    middle = pl.pallas_call(
        middle_kernel,
        out_shape=shapes,
        in_specs=[VMEM] * 3 + [HBM] * 3,
        out_specs=[HBM] * 2,
        scratch_shapes=[
            pltpu.VMEM((D, D), BF16),
            pltpu.VMEM((D, FF), BF16),
            pltpu.VMEM((FF, D), BF16),
            pltpu.VMEM((CELLS - 2 * HALO, D), BF16),
            pltpu.SemaphoreType.DMA((3,)),
            pltpu.SemaphoreType.DMA((4,)),
            pltpu.SemaphoreType.DMA,
        ],
        compiler_params=PARAMS,
        name="middle",
    )
    edges = pl.pallas_call(
        edges_kernel,
        out_shape=shapes,
        in_specs=[VMEM] * 7 + [HBM] * 2 + [pl.BlockSpec(memory_space=pltpu.SMEM)],
        out_specs=[HBM] * 2,
        input_output_aliases={7: 0, 8: 1},
        scratch_shapes=[pltpu.VMEM((2 * HALO, D), BF16), pltpu.SemaphoreType.DMA((4,))],
        compiler_params=PARAMS,
        name="edges",
    )
    partly, partly_sent = middle(
        state,
        noise[0],
        neighbours,
        in_hbm(msg_weight),
        in_hbm(up_weight),
        in_hbm(down_weight),
    )
    teacher, sent = edges(
        far,
        near,
        state,
        neighbours,
        msg_weight,
        up_weight,
        down_weight,
        partly,
        partly_sent,
        odd.astype(jnp.int32).reshape(1),
    )
    every = lax.all_to_all(
        sent.reshape(MEMBERS, BLOCK, D + NOISE),
        MEMBER,
        split_axis=0,
        concat_axis=0,
        tiled=True,
    )
    mine = mine.reshape(CELLS, D)
    pupil = pl.pallas_call(
        student_kernel,
        out_shape=(
            jax.ShapeDtypeStruct((CELLS, H), F32),
            jax.ShapeDtypeStruct((D, CELLS), BF16),
        ),
        in_specs=[VMEM] * 2,
        out_specs=[VMEM] * 2,
        compiler_params=PARAMS,
        name="student",
    )
    early, turned = pupil(mine, student_in)
    place = jnp.stack([region_map[0], lax.axis_index("core").astype(jnp.int32)])
    send, keep = pl.pallas_call(
        score_kernel,
        out_shape=[jax.ShapeDtypeStruct((XY, 2, SHARE, 128), BF16)] * 2,
        in_specs=[VMEM] * 5 + [HBM, pl.BlockSpec(memory_space=pltpu.SMEM)],
        out_specs=[VMEM] * 2,
        scratch_shapes=[
            pltpu.VMEM((MEMBERS, BLOCK, D), BF16),
            pltpu.VMEM((CELLS, D), BF16),
            pltpu.VMEM((16, 128), F32),
            pltpu.VMEM((D, CELLS), BF16),
            pltpu.VMEM((NOISE, CELLS), BF16),
            pltpu.VMEM((H, CELLS), BF16),
            pltpu.VMEM((CELLS, H), F32),
            pltpu.VMEM((CELLS, D), BF16),
            pltpu.SemaphoreType.DMA,
        ],
        compiler_params=PARAMS,
        name="score",
    )(early, mine, every, student_noise, student_out, in_hbm(turned), place)
    other = lax.ppermute(send, "core", [(0, 1), (1, 0)])
    half = (keep.astype(F32) + other.astype(F32)).astype(BF16)
    shares = lax.all_to_all(half, ("tile_1", "tile_2"), split_axis=0, concat_axis=0, tiled=True)
    copies = pl.pallas_call(
        fold_kernel,
        out_shape=jax.ShapeDtypeStruct((2 * MEMBERS, SHARE, 128), BF16),
        in_specs=[VMEM],
        out_specs=VMEM,
        compiler_params=PARAMS,
        name="fold",
    )(shares)
    parts = lax.all_to_all(
        copies, ("tile_0", "member_0", "core"), split_axis=0, concat_axis=0, tiled=True
    )
    region_loss, grad_in, grad_noise, grad_out = pl.pallas_call(
        last_kernel,
        out_shape=[
            jax.ShapeDtypeStruct((1, REGIONS), F32),
            jax.ShapeDtypeStruct((8, D), F32),
            jax.ShapeDtypeStruct((2, D), F32),
            jax.ShapeDtypeStruct((8, D), F32),
        ],
        in_specs=[VMEM],
        out_specs=[VMEM] * 4,
        compiler_params=PARAMS,
        name="last",
    )(parts)
    return (teacher[None], region_loss.reshape(REGIONS), grad_in, grad_noise, grad_out)


def solution(mesh):
    split = Mesh(
        mesh.devices.reshape(4, 2, 2, 4, 8), ("member_0", "core", "tile_0", "tile_1", "tile_2")
    )
    in_specs = (
        P(MEMBER, TILE, None),
        P(MEMBER, TILE, None),
        P(None, TILE),
        P(TILE),
        P(),
        P(),
        P(),
        P(),
        P(),
        P(),
    )
    out_specs = (P(MEMBER, TILE, None), P(), P(TILE, None), P(TILE, None), P(TILE, None))
    return jax.shard_map(step, mesh=split, in_specs=in_specs, out_specs=out_specs, check_vma=False)
```
